32 devices in a mesh: ens: 2 (over x), lat: 16 (over z, y, core).
Axes of the slice: x: 2, y: 2, z: 4, core: 2. Of those that a mesh axis runs over, the one named last changes fastest.
Arguments:
- state: bfloat16 [256, 1440, 128], P(('ens', 'lat')), parts along dimension 0, may hold values from -6 to 6
- inner_weight: bfloat16 [2, 1152, 512], replicated, may hold values from -0.1875 to 0.1875
- outer_weight: bfloat16 [2, 512, 128], replicated, may hold values from -0.25 to 0.25
- surface_proj: bfloat16 [2, 128, 4], replicated, may hold values from -0.5 to 0.5
- forcing_in: bfloat16 [2, 4, 512], replicated, may hold values from -3 to 3
- margin_rows: int32 [2, 64, 3], replicated, may hold values from 0 to 63, as said below
- margin_weights: float32 [2, 64, 3], replicated, may hold values from 0.2 to 1
- wet_mask: int32 [64, 1440], replicated, may hold values 0 or 1
Outputs:
- next_state: bfloat16 [256, 1440, 128], P(('ens', 'lat')), parts along dimension 0
The draws below stay inside these ranges and needn't reach their ends.
There are 2 independent parts, one for each index of `ens`. The reference program is written for one: setup_inputs(seed, part) draws one part's arguments, and reference() takes and returns one part's arrays. A program takes and returns all parts, laid end to end along the dimension named above; an argument that names none is the same for every part. Nothing has to cross between parts.
Inputs may be any that keep to these rules, and one draw needn't show every extreme that they name: `margin_rows`: every entry of row r of either component lies between ((r) // 8 - 1) * 8 and ((r) // 8 + 2) * 8 - 1 (within 0 to 63); r + k * 8 with k = -1 is reached by the first row of each block of 8 rows and k = 1 plus 8 - 1 by the last, unless the component ends there.
All inputs are finite; a program needn't handle non-finite values.
Results may differ from the reference program's by a relative error of at most 0.0085.
Values may be sent and summed in bfloat16 or wider, within the bound.
No kernel may reach another device: no remote copies, remote signals or barrier semaphores. Data moves between devices by JAX's collectives and lax.ppermute only.
A program may use at most 128 MiB of HBM per device.

```python
import math
import jax
import jax.numpy as jnp
from jax import lax

LON = 1440
CH = 128
HID = 512
NF = 4
MARGINS = 3
ROWS = 8
COMP_ROWS = 64


def draw_margin_rows(key, part):
    row_ids = jnp.arange(COMP_ROWS, dtype=jnp.int32)
    within = row_ids % ROWS
    offsets = jax.random.randint(jax.random.fold_in(key, 17), (2, COMP_ROWS, MARGINS), -ROWS, ROWS + 1, dtype=jnp.int32)
    first = jnp.where(within[None, :] == 0, -ROWS, offsets[:, :, 0])
    last = jnp.where(within[None, :] == ROWS - 1, ROWS, offsets[:, :, MARGINS - 1])
    offsets = offsets.at[:, :, 0].set(first)
    offsets = offsets.at[:, :, MARGINS - 1].set(last)
    table = row_ids[None, :, None] + offsets
    return jnp.clip(table, 0, COMP_ROWS - 1).astype(jnp.int32)


def with_ends(entries, stream_key, least, high):
    extent = entries.shape
    index_at = [jax.random.randint(jax.random.fold_in(stream_key, axis), (), 0, extent[axis]) for axis in range(len(extent))]
    entries = entries.at[tuple(index_at)].set(least)
    longest = extent.index(max(extent))
    index_at[longest] = (index_at[longest] + 1) % extent[longest]
    return entries.at[tuple(index_at)].set(high)


def block_levels(own_key, dims, pieces, least, high):
    def one(dim, blocks):
        draws = jax.random.uniform(jax.random.fold_in(jax.random.fold_in(own_key, 6), dim), (blocks,), jnp.float32, least / len(pieces), high / len(pieces))
        return jnp.repeat(jnp.exp(draws), dims[dim] // blocks).reshape((-1,) + (1,) * (len(dims) - dim - 1))

    gain = one(*pieces[0])
    for cut in pieces[1:]:
        gain = gain * one(*cut)
    return gain


def normal_values(rng, extent, scale, limit, split=(), held_as=jnp.bfloat16):
    entries = scale * jax.random.normal(rng, extent, jnp.float32)
    if split:
        entries = entries * block_levels(rng, extent, split, -0.22, 0.18)
    return jnp.clip(entries, -limit, limit).astype(held_as)


def setup_inputs(seed: int = 0, part: int = 0) -> dict:
    seeds = jax.random.split(jax.random.key(seed), 9)
    own_keys = jax.random.split(jax.random.fold_in(seeds[8], part), 9)
    return {
        "state": normal_values(own_keys[0], (2 * COMP_ROWS, LON, CH), 1.0, 6.0, ((0, 16),)),
        "inner_weight": normal_values(seeds[1], (2, 9 * CH, HID), (9 * CH) ** -0.5, 0.1875),
        "outer_weight": normal_values(seeds[2], (2, HID, CH), HID ** -0.5, 0.25),
        "surface_proj": normal_values(seeds[3], (2, CH, NF), CH ** -0.5, 0.5),
        "forcing_in": normal_values(seeds[4], (2, NF, HID), NF ** -0.5, 3.0),
        "margin_rows": draw_margin_rows(jax.random.fold_in(seeds[8], 71), part),
        "margin_weights": jnp.clip(jnp.exp(jax.random.uniform(seeds[6], (2, COMP_ROWS, MARGINS), jnp.float32, math.log(0.2), math.log(1.0))), 0.2, 1.0),
        "wet_mask": with_ends((jax.random.randint(seeds[7], (COMP_ROWS, LON), 0, 3) < 2).astype(jnp.int32), jax.random.fold_in(seeds[7], 1), 0, 1),
    }


def component_step(current, forcing, inner, forcing_map, outer, wet_factor):
    padded = jnp.pad(current, ((1, 1), (0, 0), (0, 0)))
    forcing_blocks = forcing.reshape(COMP_ROWS, NF, LON)
    forcing_map32 = forcing_map.astype(jnp.float32)

    def one_row(row_number):
        window = lax.dynamic_slice_in_dim(padded, row_number, 3, 0)
        pieces_list = []
        for row_shift in range(3):
            for lon_shift in range(3):
                pieces_list.append(jnp.roll(window[row_shift], 1 - lon_shift, axis=0))
        patch = jnp.concatenate(pieces_list, axis=-1)
        pre_act = jnp.dot(patch, inner, preferred_element_type=jnp.float32)
        pre_act = pre_act + jnp.einsum("fl,fh->lh", forcing_blocks[row_number], forcing_map32)
        hidden = jax.nn.silu(pre_act).astype(jnp.bfloat16)
        return jnp.dot(hidden, outer, preferred_element_type=jnp.float32)

    update = lax.map(one_row, jnp.arange(COMP_ROWS, dtype=jnp.int32))
    result = (current.astype(jnp.float32) + update) * wet_factor[:, :, None]
    return result.astype(jnp.bfloat16)


def make_surface(current, proj, wet_factor):
    values = jnp.einsum("rlc,cf->rfl", current.astype(jnp.float32), proj.astype(jnp.float32))
    values = values * wet_factor[:, None, :]
    return values.astype(jnp.bfloat16).reshape(COMP_ROWS, NF * LON)


def regrid(surface_other, table, fractions):
    picked = surface_other[table].astype(jnp.float32)
    return jnp.einsum("rk,rkx->rx", fractions, picked)


def reference(state, inner_weight, outer_weight, surface_proj, forcing_in, margin_rows, margin_weights, wet_mask):
    shifted = jnp.roll(state, COMP_ROWS // 2, axis=0)
    atmos = shifted[:COMP_ROWS]
    ocean = shifted[COMP_ROWS:]
    wet = wet_mask.astype(jnp.float32)
    ones_field = jnp.ones((COMP_ROWS, LON), jnp.float32)
    surface_atm = make_surface(atmos, surface_proj[0], ones_field)
    surface_ocn = make_surface(ocean, surface_proj[1], wet)
    forcing_atm = regrid(surface_ocn, margin_rows[0], margin_weights[0])
    forcing_ocn = regrid(surface_atm, margin_rows[1], margin_weights[1])
    next_atm = component_step(atmos, forcing_atm, inner_weight[0], forcing_in[0], outer_weight[0], ones_field)
    next_ocn = component_step(ocean, forcing_ocn, inner_weight[1], forcing_in[1], outer_weight[1], wet)
    new_rows = jnp.concatenate([next_atm, next_ocn], axis=0)
    return jnp.roll(new_rows, -(COMP_ROWS // 2), axis=0)
```

```python
import functools

import jax
import jax.numpy as jnp
from jax import lax
from jax.experimental import pallas as pl
from jax.experimental.pallas import tpu as pltpu
from jax.sharding import PartitionSpec as P

BF = jnp.bfloat16
F32 = jnp.float32
GROUPS = 4
FIRST_PAIRS = 2


def dot(a, b):
    return jnp.dot(a, b, preferred_element_type=F32)


def lane(shape):
    return lax.broadcasted_iota(jnp.int32, shape, len(shape) - 1)


def sublane(shape):
    return lax.broadcasted_iota(jnp.int32, shape, len(shape) - 2)


def limits(mib):
    return pltpu.CompilerParams(
        dimension_semantics=("arbitrary",), vmem_limit_bytes=mib << 20
    )


def surface_kernel(rows, lon, group, fluxes, where, x_ref, proj_ref, wet_ref, out_ref, acc, wetf):
    step = pl.program_id(0)
    channels = x_ref.shape[2]
    spread = (lane((fluxes, 128)) % fluxes == sublane((fluxes, 128))).astype(BF)
    tiled = dot(proj_ref[0], spread).astype(BF)

    @pl.when(step == 0)
    def _():
        acc[...] = jnp.zeros_like(acc)

    owner = lane((channels, 128)) // fluxes
    for g in range(GROUPS):
        size = min(group, lon - g * group)
        span = slice(g * group, g * group + size)
        lhs = jnp.concatenate([x_ref[0, span, :], x_ref[1, span, :]], axis=1)
        halves = [
            jnp.where(owner == g * rows + 2 * step + k, tiled, jnp.zeros_like(tiled)) for k in (0, 1)
        ]
        acc[0:size, :] += dot(lhs, jnp.concatenate(halves, axis=0))

    @pl.when(step == pl.num_programs(0) - 1)
    def _():
        wetf[...] = jnp.zeros_like(wetf)
        wetf[:, 0:lon] = wet_ref[...].astype(F32)
        mask = jnp.zeros_like(acc)
        for g in range(GROUPS):
            pick = (lane((rows, 128)) // fluxes == g * rows + sublane((rows, 128))).astype(F32)
            mask += lax.dot_general(
                wetf[:, g * group : (g + 1) * group], pick, (((0,), (0,)), ((), ())),
                preferred_element_type=F32,
            )
        mask = jnp.where(where[0] == 1, mask, jnp.ones_like(mask))
        out_ref[...] = (acc[...] * mask).astype(BF)


def surfaces(where, state, surface_proj, wet_mask, group):
    rows, lon, channels = state.shape
    fluxes = surface_proj.shape[2]
    return pl.pallas_call(
        functools.partial(surface_kernel, rows, lon, group, fluxes),
        grid_spec=pltpu.PrefetchScalarGridSpec(
            num_scalar_prefetch=1,
            grid=(rows // 2,),
            in_specs=[
                pl.BlockSpec((2, lon, channels), lambda i, s: (i, 0, 0)),
                pl.BlockSpec((1, channels, fluxes), lambda i, s: (s[0], 0, 0)),
                pl.BlockSpec((rows, lon), lambda i, s: (s[1], 0)),
            ],
            out_specs=pl.BlockSpec((group, 128), lambda i, s: (0, 0)),
            scratch_shapes=[
                pltpu.VMEM((group, 128), F32),
                pltpu.VMEM((rows, GROUPS * group), F32),
            ],
        ),
        out_shape=jax.ShapeDtypeStruct((group, 128), BF),
        compiler_params=limits(16),
        name="surface_fields",
    )(where, state, surface_proj, wet_mask)


def partial_kernel(first, pairs, lon, edges, *refs):
    if edges:
        where, d0, d1, d2, d3, w_ref, low_ref, high_ref, out_ref, up_ref, down_ref, tf, wy, wm = refs
    else:
        where, d0, d1, d2, d3, w_ref, _, out_ref, tf, wy, wm = refs
    step = pl.program_id(0)
    pair = step + first

    def tap(a, b):
        return w_ref[0, pl.ds((a * 3 + b) * 128, 128), :].astype(F32) * 0.5

    @pl.when(step == 0)
    def _():
        for k, (a, b) in enumerate(((0, 0), (0, 2), (1, 1), (2, 1))):
            wy[0, k * 128 : (k + 1) * 128, :] = tap(a, b).astype(BF)
        for k, (a, b) in enumerate(((2, 0), (2, 2), (0, 1), (1, 1))):
            wy[1, k * 128 : (k + 1) * 128, :] = tap(a, b).astype(BF)
        for k, b in enumerate((0, 2)):
            ends = tap(0, b) + tap(2, b)
            wm[0, k * 128 : (k + 1) * 128, :] = (0.5 * (ends + tap(1, b))).astype(BF)
            wm[1, k * 128 : (k + 1) * 128, :] = (0.5 * (ends - tap(1, b))).astype(BF)
        if edges:
            up_ref[0:lon, :] = high_ref[0]
            down_ref[0:lon, :] = low_ref[0]

    south = jnp.where(pair == 0, 0.0, 1.0)
    north = jnp.where(pair == pairs - 1, 0.0, 1.0)
    x1 = d1[0].astype(F32)
    x2 = d2[0].astype(F32)
    for p, t in enumerate(
        (d0[0].astype(F32) * south - x2, x1 + x2, x2 - x1, d3[0].astype(F32) * north - x1)
    ):
        tf[p, 8 : 8 + lon, :] = t
        tf[p, 7:8, :] = t[lon - 1 : lon]
        tf[p, 8 + lon : 9 + lon, :] = t[0:1]

    def sides(p):
        return [tf[p, 7 : 7 + lon, :].astype(BF), tf[p, 9 : 9 + lon, :].astype(BF)]

    own = [d1[0], d2[0]]
    m1 = dot(jnp.concatenate(sides(1), axis=1), wm[0])
    m2 = dot(jnp.concatenate(sides(2), axis=1), wm[1])
    out_ref[0] = (dot(jnp.concatenate(sides(0) + own, axis=1), wy[0]) + (m1 + m2)).astype(BF)
    out_ref[1] = (dot(jnp.concatenate(sides(3) + own, axis=1), wy[1]) + (m1 - m2)).astype(BF)


def partials(where, state, inner_weight, first, count, group, earlier=None):
    rows, lon, channels = state.shape
    depth, hidden = inner_weight.shape[1:]
    edges = earlier is None

    def row(offset):
        def index(i, s):
            return (jnp.clip(2 * (i + first) + offset, 0, rows - 1), 0, 0)

        return pl.BlockSpec((1, lon, channels), index)

    in_specs = [row(k) for k in (-1, 0, 1, 2)]
    in_specs.append(pl.BlockSpec((1, depth, hidden), lambda i, s: (s[0], 0, 0)))
    out_specs = [pl.BlockSpec((2, lon, hidden), lambda i, s: (i + first, 0, 0))]
    out_shape = [jax.ShapeDtypeStruct((rows, lon, hidden), BF)]
    operands = [state] * 4 + [inner_weight]
    aliases = {}
    if edges:
        in_specs.append(pl.BlockSpec((1, lon, channels), lambda i, s: (0, 0, 0)))
        in_specs.append(pl.BlockSpec((1, lon, channels), lambda i, s: (rows - 1, 0, 0)))
        operands += [state, state]
        for _ in range(2):
            out_specs.append(pl.BlockSpec((lon + group, channels), lambda i, s: (0, 0)))
            out_shape.append(jax.ShapeDtypeStruct((lon + group, channels), BF))
    else:
        in_specs.append(pl.BlockSpec(memory_space=pl.ANY))
        operands.append(earlier)
        aliases = {6: 0}
    return pl.pallas_call(
        functools.partial(partial_kernel, first, rows // 2, lon, edges),
        grid_spec=pltpu.PrefetchScalarGridSpec(
            num_scalar_prefetch=1,
            grid=(count,),
            in_specs=in_specs,
            out_specs=out_specs,
            scratch_shapes=[
                pltpu.VMEM((4, lon + 16, channels), F32),
                pltpu.VMEM((2, 4 * channels, hidden), BF),
                pltpu.VMEM((2, 2 * channels, hidden), BF),
            ],
        ),
        out_shape=out_shape,
        input_output_aliases=aliases,
        compiler_params=limits(52),
        cost_estimate=pl.CostEstimate(
            flops=count * 2 * lon * 6 * channels * hidden * 2,
            bytes_accessed=count * 2 * lon * (hidden + 2 * channels) * 2,
            transcendentals=0,
        ),
        name="own_rows",
    )(where, *operands)


def finish_kernel(
    rows, lon, group, fluxes, where, x_ref, near_ref, part_ref, low_ref, high_ref, mid_ref, wl_ref, wh_ref,
    f_ref, o_ref, wet_ref, table, weights, out_ref, halo, window, we, spread, wett, wetf,
):
    r = pl.program_id(0)
    parity = r % 2

    @pl.when(r == 0)
    def _():
        for e, (side, w_ref) in enumerate(((low_ref, wl_ref), (high_ref, wh_ref))):
            v = side[0:lon, :].astype(F32)
            halo[e, 8 : 8 + lon, :] = v
            halo[e, 7:8, :] = v[lon - 1 : lon]
            halo[e, 8 + lon : 9 + lon, :] = v[0:1]
            for k, b in enumerate((0, 2, 1)):
                tap = w_ref[0, b * 128 : (b + 1) * 128, :].astype(F32) * 0.5
                we[e, k * 128 : (k + 1) * 128, :] = tap.astype(BF)
        packs = [
            low_ref[lon : lon + group, :].astype(F32),
            mid_ref[...].astype(F32),
            high_ref[lon : lon + group, :].astype(F32),
        ]
        for g in range(GROUPS):
            size = min(group, lon - g * group)
            held = lane((group, 128)) // (rows * fluxes)
            total = jnp.zeros((group, 128), F32)
            for w, pack in enumerate(packs):
                shift = (rows * fluxes * (w - g)) % 128
                moved = pltpu.roll(pack, shift, 1) if shift else pack
                total = jnp.where(held == w, moved, total)
            window[g * group : g * group + size, :] = total[0:size].astype(BF)
        at = sublane((128, spread.shape[1])) % fluxes
        total = jnp.zeros(spread.shape, F32)
        for f in range(fluxes):
            total = jnp.where(at == f, f_ref[0, f : f + 1, :].astype(F32) * 0.5, total)
        spread[...] = total
        wetf[...] = jnp.zeros_like(wetf)
        wetf[0:rows, 0:lon] = jnp.where(where[0] == 1, wet_ref[...].astype(F32), 1.0)
        for c in range(wetf.shape[1] // 128):
            wett[c * 128 : (c + 1) * 128, :] = wetf[:, c * 128 : (c + 1) * 128].T

    slot = sublane(spread.shape) // fluxes
    share = jnp.zeros(spread.shape, F32)
    for m in range(table.shape[2]):
        local = table[0, r, m] - (where[1] - 1) * rows
        share += jnp.where(slot == local, weights[0, r, m], 0.0)
    we[parity, 384:512, :] = (share * spread[...]).astype(BF)

    def close(total):
        total = total + part_ref[0].astype(F32)
        act = (total + total * jnp.tanh(total)).astype(BF)
        value = x_ref[0].astype(F32) + dot(act, o_ref[0])
        pick = lane((lon, 128)) == r
        keep = jnp.max(jnp.where(pick, wett[0:lon, :], 0.0), axis=1, keepdims=True)
        out_ref[0] = jnp.where(keep > 0.5, value, 0.0).astype(BF)

    edge = jnp.logical_or(r == 0, r == rows - 1)

    @pl.when(edge)
    def _():
        lhs = [halo[parity, k : k + lon, :].astype(BF) for k in (7, 9, 8)] + [window[...]]
        close(dot(jnp.concatenate(lhs, axis=1), we[parity]))

    @pl.when(jnp.logical_not(edge))
    def _():
        close(dot(jnp.concatenate([near_ref[0], window[...]], axis=1), we[parity, 256:512, :]))


def finish(where, state, part, low, high, mid, inner_weight, forcing_in, outer_weight, wet_mask, table, weights):
    rows, lon, channels = state.shape
    hidden = inner_weight.shape[2]
    fluxes = forcing_in.shape[1]
    group = mid.shape[0]
    margins = table.shape[2]

    def near(r, s):
        return (jnp.clip(r - 1 + 2 * (r % 2), 0, rows - 1), 0, 0)

    def whole(i, s):
        return (0, 0)

    return pl.pallas_call(
        functools.partial(finish_kernel, rows, lon, group, fluxes),
        grid_spec=pltpu.PrefetchScalarGridSpec(
            num_scalar_prefetch=1,
            grid=(rows,),
            in_specs=[
                pl.BlockSpec((1, lon, channels), lambda r, s: (r, 0, 0)),
                pl.BlockSpec((1, lon, channels), near),
                pl.BlockSpec((1, lon, hidden), lambda r, s: (r, 0, 0)),
                pl.BlockSpec((lon + group, channels), whole),
                pl.BlockSpec((lon + group, channels), whole),
                pl.BlockSpec((group, channels), whole),
                pl.BlockSpec((1, 3 * channels, hidden), lambda r, s: (s[0], 0, 0)),
                pl.BlockSpec((1, 3 * channels, hidden), lambda r, s: (s[0], 2, 0)),
                pl.BlockSpec((1, fluxes, hidden), lambda r, s: (s[0], 0, 0)),
                pl.BlockSpec((1, hidden, channels), lambda r, s: (s[0], 0, 0)),
                pl.BlockSpec((rows, lon), lambda r, s: (s[1], 0)),
                pl.BlockSpec((1, rows, margins), lambda r, s: (s[0], s[1], 0), memory_space=pltpu.SMEM),
                pl.BlockSpec((1, rows, margins), lambda r, s: (s[0], s[1], 0), memory_space=pltpu.SMEM),
            ],
            out_specs=pl.BlockSpec((1, lon, channels), lambda r, s: (r, 0, 0)),
            scratch_shapes=[
                pltpu.VMEM((2, lon + 16, channels), F32),
                pltpu.VMEM((lon, 128), BF),
                pltpu.VMEM((2, 512, hidden), BF),
                pltpu.VMEM((128, hidden), F32),
                pltpu.VMEM((GROUPS * group, 128), F32),
                pltpu.VMEM((128, GROUPS * group), F32),
            ],
        ),
        out_shape=jax.ShapeDtypeStruct((rows, lon, channels), BF),
        compiler_params=limits(52),
        name="finish_rows",
    )(
        where, state, state, part, low, high, mid, inner_weight, inner_weight, forcing_in, outer_weight,
        wet_mask, table, weights,
    )


def shards(state, inner_weight, outer_weight, surface_proj, forcing_in, margin_rows, margin_weights, wet_mask):
    count = lax.axis_size("lat")
    half = count // 2
    quarter = half // 2
    lon = state.shape[1]
    group = -(-lon // (GROUPS * 128)) * 128
    moved = (lax.axis_index("lat") + quarter) % count
    where = jnp.where(lax.iota(jnp.int32, 2) == 0, moved // half, moved % half)

    def component(i):
        return ((i + quarter) % count) // half

    def beside(block, distance):
        route = [(i, (i + distance) % count) for i in range(count)]
        route = [(i, j) for i, j in route if component(i) == component(j)]
        return lax.ppermute(block, "lat", route)

    pack = surfaces(where, state, surface_proj, wet_mask, group)
    mid = lax.ppermute(pack, "lat", [(i, (i + half) % count) for i in range(count)])
    part, up, down = partials(where, state, inner_weight, 0, FIRST_PAIRS, group)
    mid, part = lax.optimization_barrier((mid, part))
    up = lax.dynamic_update_slice(up, mid, (lon, 0))
    down = lax.dynamic_update_slice(down, mid, (lon, 0))
    low = beside(up, 1)
    high = beside(down, -1)
    (part,) = partials(
        where, state, inner_weight, FIRST_PAIRS, state.shape[0] // 2 - FIRST_PAIRS, group, part
    )
    return finish(
        where, state, part, low, high, mid, inner_weight, forcing_in, outer_weight, wet_mask,
        margin_rows, margin_weights,
    )


def solution(mesh):
    placed = (P(("ens", "lat"), None, None), P(), P(), P(), P(), P(), P(), P())
    return jax.shard_map(
        shards, mesh=mesh, in_specs=placed, out_specs=P(("ens", "lat"), None, None), check_vma=False
    )
```

```python
import functools

import jax
import jax.numpy as jnp
from jax import lax
from jax.experimental import pallas as pl
from jax.experimental.pallas import tpu as pltpu
from jax.sharding import PartitionSpec as P

BF = jnp.bfloat16
F32 = jnp.float32
GROUPS = 4
FIRST_PAIRS = 2


def dot(a, b):
    return jnp.dot(a, b, preferred_element_type=F32)


def lane(shape):
    return lax.broadcasted_iota(jnp.int32, shape, len(shape) - 1)


def sublane(shape):
    return lax.broadcasted_iota(jnp.int32, shape, len(shape) - 2)


def limits(mib):
    return pltpu.CompilerParams(
        dimension_semantics=("arbitrary",), vmem_limit_bytes=mib << 20
    )


def surface_kernel(
    rows, lon, group, fluxes, where, x_ref, proj_ref, wet_ref, out_ref, xv_ref, up_ref, down_ref, acc, wetf
):
    step = pl.program_id(0)
    channels = x_ref.shape[2]
    spread = (lane((fluxes, 128)) % fluxes == sublane((fluxes, 128))).astype(BF)
    tiled = lax.dot_general(
        proj_ref[0], spread, (((0,), (0,)), ((), ())), preferred_element_type=F32
    ).astype(BF)
    xv_ref[2 * step] = x_ref[0]
    xv_ref[2 * step + 1] = x_ref[1]

    @pl.when(step == 0)
    def _():
        acc[...] = jnp.zeros_like(acc)
        down_ref[0:lon, :] = x_ref[0]

    owner = lane((channels, 128)) // fluxes
    for g in range(GROUPS):
        size = min(group, lon - g * group)
        span = slice(g * group, g * group + size)
        lhs = jnp.concatenate([x_ref[0, span, :], x_ref[1, span, :]], axis=1)
        halves = [
            jnp.where(owner == g * rows + 2 * step + k, tiled, jnp.zeros_like(tiled)) for k in (0, 1)
        ]
        acc[0:size, :] += dot(lhs, jnp.concatenate(halves, axis=0))

    @pl.when(step == pl.num_programs(0) - 1)
    def _():
        up_ref[0:lon, :] = x_ref[1]
        wetf[...] = jnp.zeros_like(wetf)
        wetf[:, 0:lon] = wet_ref[...].astype(F32)
        mask = jnp.zeros_like(acc)
        for g in range(GROUPS):
            pick = (lane((rows, 128)) // fluxes == g * rows + sublane((rows, 128))).astype(F32)
            mask += lax.dot_general(
                wetf[:, g * group : (g + 1) * group], pick, (((0,), (0,)), ((), ())),
                preferred_element_type=F32,
            )
        mask = jnp.where(where[0] == 1, mask, jnp.ones_like(mask))
        out_ref[...] = (acc[...] * mask).astype(BF)


def held():
    return pl.BlockSpec(memory_space=pltpu.VMEM)


def surfaces(where, state, surface_proj, wet_mask, group):
    rows, lon, channels = state.shape
    fluxes = surface_proj.shape[2]
    return pl.pallas_call(
        functools.partial(surface_kernel, rows, lon, group, fluxes),
        grid_spec=pltpu.PrefetchScalarGridSpec(
            num_scalar_prefetch=1,
            grid=(rows // 2,),
            in_specs=[
                pl.BlockSpec((2, lon, channels), lambda i, s: (i, 0, 0)),
                pl.BlockSpec((1, fluxes, channels), lambda i, s: (s[0], 0, 0)),
                pl.BlockSpec((rows, lon), lambda i, s: (s[1], 0)),
            ],
            out_specs=[held()] * 4,
            scratch_shapes=[
                pltpu.VMEM((group, 128), F32),
                pltpu.VMEM((rows, GROUPS * group), F32),
            ],
        ),
        out_shape=[
            pltpu.VMEM((group, 128), BF),
            pltpu.VMEM((rows, lon, channels), BF),
            pltpu.VMEM((lon + group, channels), BF),
            pltpu.VMEM((lon + group, channels), BF),
        ],
        compiler_params=limits(16),
        name="surface_fields",
    )(
        where,
        pltpu.with_memory_space_constraint(state, pltpu.HBM),
        jnp.swapaxes(surface_proj, 1, 2),
        pltpu.with_memory_space_constraint(wet_mask, pltpu.HBM),
    )


def partial_kernel(first, pairs, lon, *refs):
    if first == 0:
        where, x_ref, w_ref, out_ref, wy, wm, we, tf = refs
    else:
        where, x_ref, wy, wm, _, out_ref, tf = refs
    step = pl.program_id(0)
    pair = step + first

    if first == 0:

        def tap(a, b):
            return w_ref[0, pl.ds((a * 3 + b) * 128, 128), :].astype(F32) * 0.5

        @pl.when(step == 0)
        def _():
            for k, (a, b) in enumerate(((0, 0), (0, 2), (1, 1), (2, 1))):
                wy[0, k * 128 : (k + 1) * 128, :] = tap(a, b).astype(BF)
            for k, (a, b) in enumerate(((2, 0), (2, 2), (0, 1), (1, 1))):
                wy[1, k * 128 : (k + 1) * 128, :] = tap(a, b).astype(BF)
            for k, b in enumerate((0, 2)):
                ends = tap(0, b) + tap(2, b)
                wm[0, k * 128 : (k + 1) * 128, :] = (0.5 * (ends + tap(1, b))).astype(BF)
                wm[1, k * 128 : (k + 1) * 128, :] = (0.5 * (ends - tap(1, b))).astype(BF)
            for e, a in enumerate((0, 2)):
                for k, b in enumerate((0, 2, 1)):
                    we[e, k * 128 : (k + 1) * 128, :] = tap(a, b).astype(BF)

    south = jnp.where(pair == 0, 0.0, 1.0)
    north = jnp.where(pair == pairs - 1, 0.0, 1.0)
    x0 = x_ref[jnp.maximum(2 * pair - 1, 0)].astype(F32) * south
    x1 = x_ref[2 * pair].astype(F32)
    x2 = x_ref[2 * pair + 1].astype(F32)
    x3 = x_ref[jnp.minimum(2 * pair + 2, 2 * pairs - 1)].astype(F32) * north
    for p, t in enumerate((x0 - x2, x1 + x2, x2 - x1, x3 - x1)):
        tf[p, 8 : 8 + lon, :] = t
        tf[p, 7:8, :] = t[lon - 1 : lon]
        tf[p, 8 + lon : 9 + lon, :] = t[0:1]

    def sides(p):
        return [tf[p, 7 : 7 + lon, :].astype(BF), tf[p, 9 : 9 + lon, :].astype(BF)]

    own = [x_ref[2 * pair], x_ref[2 * pair + 1]]
    m1 = dot(jnp.concatenate(sides(1), axis=1), wm[0])
    m2 = dot(jnp.concatenate(sides(2), axis=1), wm[1])
    out_ref[2 * pair] = (dot(jnp.concatenate(sides(0) + own, axis=1), wy[0]) + (m1 + m2)).astype(BF)
    out_ref[2 * pair + 1] = (dot(jnp.concatenate(sides(3) + own, axis=1), wy[1]) + (m1 - m2)).astype(BF)


def partials(where, xv, inner_weight, first, count, earlier=None):
    rows, lon, channels = xv.shape
    depth, hidden = inner_weight.shape[1:]
    out_shape = [pltpu.VMEM((rows, lon, hidden), BF)]
    in_specs = [held()]
    if earlier is None:
        in_specs.append(pl.BlockSpec((1, depth, hidden), lambda i, s: (s[0], 0, 0), pipeline_mode=pl.Buffered(1)))
        operands = [xv, inner_weight]
        out_shape += [
            pltpu.VMEM((2, 4 * channels, hidden), BF),
            pltpu.VMEM((2, 2 * channels, hidden), BF),
            pltpu.VMEM((2, 3 * channels, hidden), BF),
        ]
        aliases = {}
    else:
        part, wy, wm = earlier
        in_specs += [held()] * 3
        operands = [xv, wy, wm, part]
        aliases = {4: 0}
    return pl.pallas_call(
        functools.partial(partial_kernel, first, rows // 2, lon),
        grid_spec=pltpu.PrefetchScalarGridSpec(
            num_scalar_prefetch=1,
            grid=(count,),
            in_specs=in_specs,
            out_specs=[held()] * len(out_shape),
            scratch_shapes=[pltpu.VMEM((4, lon + 16, channels), F32)],
        ),
        out_shape=out_shape,
        input_output_aliases=aliases,
        compiler_params=limits(28),
        cost_estimate=pl.CostEstimate(
            flops=count * 2 * lon * 6 * channels * hidden * 2,
            bytes_accessed=count * 2 * lon * (hidden + 2 * channels) * 2,
            transcendentals=0,
        ),
        name="own_rows",
    )(where, *operands)


def finish_kernel(
    rows, lon, group, fluxes, where, table, weights, x_ref, part_ref, low_ref, high_ref, mid_ref, taps_ref,
    f_ref, o_ref, wet_ref, out_ref, halo, window, we, spread, wett, wetf,
):
    r = pl.program_id(0)
    parity = r % 2

    @pl.when(r == 0)
    def _():
        we[:, 0:384, :] = taps_ref[...]
        for e, side in enumerate((low_ref, high_ref)):
            v = side[0:lon, :].astype(F32)
            halo[e, 8 : 8 + lon, :] = v
            halo[e, 7:8, :] = v[lon - 1 : lon]
            halo[e, 8 + lon : 9 + lon, :] = v[0:1]
        packs = [
            low_ref[lon : lon + group, :].astype(F32),
            mid_ref[...].astype(F32),
            high_ref[lon : lon + group, :].astype(F32),
        ]
        for g in range(GROUPS):
            size = min(group, lon - g * group)
            owner = lane((group, 128)) // (rows * fluxes)
            total = jnp.zeros((group, 128), F32)
            for w, pack in enumerate(packs):
                shift = (rows * fluxes * (w - g)) % 128
                moved = pltpu.roll(pack, shift, 1) if shift else pack
                total = jnp.where(owner == w, moved, total)
            window[g * group : g * group + size, :] = total[0:size].astype(BF)
        at = sublane((128, spread.shape[1])) % fluxes
        total = jnp.zeros(spread.shape, F32)
        for f in range(fluxes):
            total = jnp.where(at == f, f_ref[0, f : f + 1, :].astype(F32) * 0.5, total)
        spread[...] = total
        wetf[...] = jnp.zeros_like(wetf)
        wetf[0:rows, 0:lon] = jnp.where(where[0] == 1, wet_ref[...].astype(F32), 1.0)
        for c in range(wetf.shape[1] // 128):
            wett[c * 128 : (c + 1) * 128, :] = wetf[:, c * 128 : (c + 1) * 128].T

    slot = sublane(spread.shape) // fluxes
    share = jnp.zeros(spread.shape, F32)
    row = where[1] * rows + r
    for m in range(table.shape[0]):
        local = table[m, where[0], row] - (where[1] - 1) * rows
        share += jnp.where(slot == local, weights[m, where[0], row], 0.0)
    we[parity, 384:512, :] = (share * spread[...]).astype(BF)

    def close(total):
        total = total + part_ref[r].astype(F32)
        act = (total + total * jnp.tanh(total)).astype(BF)
        value = x_ref[r].astype(F32) + dot(act, o_ref[0])
        keep = jnp.broadcast_to(wett[0:lon, 0:1], value.shape)
        out_ref[0] = jnp.where(keep > 0.5, value, 0.0).astype(BF)
        wett[...] = pltpu.roll(wett[...], 127, 1)

    edge = jnp.logical_or(r == 0, r == rows - 1)

    @pl.when(edge)
    def _():
        lhs = [halo[parity, k : k + lon, :].astype(BF) for k in (7, 9, 8)] + [window[...]]
        close(dot(jnp.concatenate(lhs, axis=1), we[parity]))

    @pl.when(jnp.logical_not(edge))
    def _():
        near = x_ref[jnp.clip(r - 1 + 2 * parity, 0, rows - 1)]
        close(dot(jnp.concatenate([near, window[...]], axis=1), we[parity, 256:512, :]))


def finish(where, xv, part, low, high, mid, taps, forcing_in, outer_weight, wet_mask, table, weights):
    rows, lon, channels = xv.shape
    hidden = part.shape[2]
    fluxes = forcing_in.shape[1]
    group = mid.shape[0]
    scalars = pl.BlockSpec(memory_space=pltpu.SMEM)
    return pl.pallas_call(
        functools.partial(finish_kernel, rows, lon, group, fluxes),
        grid_spec=pltpu.PrefetchScalarGridSpec(
            num_scalar_prefetch=1,
            grid=(rows,),
            in_specs=[scalars, scalars] + [held()] * 6 + [
                pl.BlockSpec((1, fluxes, hidden), lambda r, s: (s[0], 0, 0)),
                pl.BlockSpec((1, hidden, channels), lambda r, s: (s[0], 0, 0)),
                pl.BlockSpec((rows, lon), lambda r, s: (s[1], 0)),
            ],
            out_specs=pl.BlockSpec((1, lon, channels), lambda r, s: (r, 0, 0)),
            scratch_shapes=[
                pltpu.VMEM((2, lon + 16, channels), F32),
                pltpu.VMEM((lon, 128), BF),
                pltpu.VMEM((2, 512, hidden), BF),
                pltpu.VMEM((128, hidden), F32),
                pltpu.VMEM((GROUPS * group, 128), F32),
                pltpu.VMEM((128, GROUPS * group), F32),
            ],
        ),
        out_shape=jax.ShapeDtypeStruct((rows, lon, channels), BF),
        compiler_params=limits(28),
        name="finish_rows",
    )(
        where, jnp.transpose(table, (2, 0, 1)), jnp.transpose(weights, (2, 0, 1)), xv, part, low, high, mid,
        taps, forcing_in, outer_weight, wet_mask,
    )


def shards(state, inner_weight, outer_weight, surface_proj, forcing_in, margin_rows, margin_weights, wet_mask):
    count = lax.axis_size("lat")
    half = count // 2
    quarter = half // 2
    lon = state.shape[1]
    group = -(-lon // (GROUPS * 128)) * 128
    moved = (lax.axis_index("lat") + quarter) % count
    where = jnp.where(lax.iota(jnp.int32, 2) == 0, moved // half, moved % half)

    def component(i):
        return ((i + quarter) % count) // half

    def beside(block, distance):
        route = [(i, (i + distance) % count) for i in range(count)]
        route = [(i, j) for i, j in route if component(i) == component(j)]
        return lax.ppermute(block, "lat", route)

    pack, xv, up, down = surfaces(where, state, surface_proj, wet_mask, group)
    mid = lax.ppermute(pack, "lat", [(i, (i + half) % count) for i in range(count)])
    part, wy, wm, taps = partials(where, xv, inner_weight, 0, FIRST_PAIRS)
    mid, part = lax.optimization_barrier((mid, part))
    up = lax.dynamic_update_slice(up, mid, (lon, 0))
    down = lax.dynamic_update_slice(down, mid, (lon, 0))
    low = beside(up, 1)
    high = beside(down, -1)
    (part,) = partials(
        where, xv, inner_weight, FIRST_PAIRS, state.shape[0] // 2 - FIRST_PAIRS, (part, wy, wm)
    )
    return finish(
        where, xv, part, low, high, mid, taps, forcing_in, outer_weight, wet_mask, margin_rows, margin_weights
    )


def solution(mesh):
    placed = (P(("ens", "lat"), None, None), P(), P(), P(), P(), P(), P(), P())
    return jax.shard_map(
        shards, mesh=mesh, in_specs=placed, out_specs=P(("ens", "lat"), None, None), check_vma=False
    )
```

```python
import functools

import jax
import jax.numpy as jnp
from jax import lax
from jax.experimental import pallas as pl
from jax.experimental.pallas import tpu as pltpu
from jax.sharding import PartitionSpec as P

BF = jnp.bfloat16
F32 = jnp.float32
GROUPS = 4


def dot(a, b):
    return jnp.dot(a, b, preferred_element_type=F32)


def lane(shape):
    return lax.broadcasted_iota(jnp.int32, shape, len(shape) - 1)


def sublane(shape):
    return lax.broadcasted_iota(jnp.int32, shape, len(shape) - 2)


def limits(mib):
    return pltpu.CompilerParams(
        dimension_semantics=("arbitrary",), vmem_limit_bytes=mib << 20
    )


def surface_kernel(
    rows, lon, group, fluxes, where, x_ref, proj_ref, wet_ref, out_ref, xv_ref, up_ref, down_ref, acc, wetf
):
    step = pl.program_id(0)
    channels = x_ref.shape[2]
    spread = (lane((fluxes, 128)) % fluxes == sublane((fluxes, 128))).astype(BF)
    tiled = lax.dot_general(
        proj_ref[0], spread, (((0,), (0,)), ((), ())), preferred_element_type=F32
    ).astype(BF)
    xv_ref[2 * step] = x_ref[0]
    xv_ref[2 * step + 1] = x_ref[1]

    @pl.when(step == 0)
    def _():
        acc[...] = jnp.zeros_like(acc)
        down_ref[...] = x_ref[0]

    owner = lane((channels, 128)) // fluxes
    for g in range(GROUPS):
        size = min(group, lon - g * group)
        span = slice(g * group, g * group + size)
        lhs = jnp.concatenate([x_ref[0, span, :], x_ref[1, span, :]], axis=1)
        halves = [
            jnp.where(owner == g * rows + 2 * step + k, tiled, jnp.zeros_like(tiled)) for k in (0, 1)
        ]
        acc[0:size, :] += dot(lhs, jnp.concatenate(halves, axis=0))

    @pl.when(step == pl.num_programs(0) - 1)
    def _():
        up_ref[...] = x_ref[1]
        wetf[...] = jnp.zeros_like(wetf)
        wetf[:, 0:lon] = wet_ref[...].astype(F32)
        mask = jnp.zeros_like(acc)
        for g in range(GROUPS):
            pick = (lane((rows, 128)) // fluxes == g * rows + sublane((rows, 128))).astype(F32)
            mask += lax.dot_general(
                wetf[:, g * group : (g + 1) * group], pick, (((0,), (0,)), ((), ())),
                preferred_element_type=F32,
            )
        mask = jnp.where(where[0] == 1, mask, jnp.ones_like(mask))
        out_ref[...] = (acc[...] * mask).astype(BF)


def in_hbm(x):
    return pltpu.with_memory_space_constraint(x, pltpu.HBM)


def held():
    return pl.BlockSpec(memory_space=pltpu.VMEM)


def surfaces(where, state, surface_proj, wet_mask, group):
    rows, lon, channels = state.shape
    fluxes = surface_proj.shape[2]
    return pl.pallas_call(
        functools.partial(surface_kernel, rows, lon, group, fluxes),
        grid_spec=pltpu.PrefetchScalarGridSpec(
            num_scalar_prefetch=1,
            grid=(rows // 2,),
            in_specs=[
                pl.BlockSpec((2, lon, channels), lambda i, s: (i, 0, 0)),
                pl.BlockSpec((1, fluxes, channels), lambda i, s: (s[0], 0, 0)),
                pl.BlockSpec((rows, lon), lambda i, s: (s[1], 0)),
            ],
            out_specs=[held()] * 4,
            scratch_shapes=[
                pltpu.VMEM((group, 128), F32),
                pltpu.VMEM((rows, GROUPS * group), F32),
            ],
        ),
        out_shape=[
            pltpu.VMEM((group, 128), BF),
            pltpu.VMEM((rows, lon, channels), BF),
            pltpu.VMEM((lon, channels), BF),
            pltpu.VMEM((lon, channels), BF),
        ],
        compiler_params=limits(16),
        name="surface_fields",
    )(
        where, in_hbm(state), in_hbm(jnp.swapaxes(surface_proj, 1, 2)), in_hbm(wet_mask)
    )


def partial_kernel(pairs, lon, where, x_ref, w_ref, out_ref, we, wy, wm, tf):
    pair = pl.program_id(0)

    def tap(a, b):
        return w_ref[0, pl.ds((a * 3 + b) * 128, 128), :].astype(F32) * 0.5

    @pl.when(pair == 0)
    def _():
        for k, (a, b) in enumerate(((0, 0), (0, 2), (1, 1), (2, 1))):
            wy[0, k * 128 : (k + 1) * 128, :] = tap(a, b).astype(BF)
        for k, (a, b) in enumerate(((2, 0), (2, 2), (0, 1), (1, 1))):
            wy[1, k * 128 : (k + 1) * 128, :] = tap(a, b).astype(BF)
        for k, b in enumerate((0, 2)):
            ends = tap(0, b) + tap(2, b)
            wm[0, k * 128 : (k + 1) * 128, :] = (0.5 * (ends + tap(1, b))).astype(BF)
            wm[1, k * 128 : (k + 1) * 128, :] = (0.5 * (ends - tap(1, b))).astype(BF)
        for e, a in enumerate((0, 2)):
            for k, b in enumerate((0, 2, 1)):
                we[e, k * 128 : (k + 1) * 128, :] = tap(a, b).astype(BF)

    south = jnp.where(pair == 0, 0.0, 1.0)
    north = jnp.where(pair == pairs - 1, 0.0, 1.0)
    x0 = x_ref[jnp.maximum(2 * pair - 1, 0)].astype(F32) * south
    x1 = x_ref[2 * pair].astype(F32)
    x2 = x_ref[2 * pair + 1].astype(F32)
    x3 = x_ref[jnp.minimum(2 * pair + 2, 2 * pairs - 1)].astype(F32) * north
    for p, t in enumerate((x0 - x2, x1 + x2, x2 - x1, x3 - x1)):
        tf[p, 8 : 8 + lon, :] = t
        tf[p, 7:8, :] = t[lon - 1 : lon]
        tf[p, 8 + lon : 9 + lon, :] = t[0:1]

    def sides(p):
        return [tf[p, 7 : 7 + lon, :].astype(BF), tf[p, 9 : 9 + lon, :].astype(BF)]

    own = [x_ref[2 * pair], x_ref[2 * pair + 1]]
    m1 = dot(jnp.concatenate(sides(1), axis=1), wm[0])
    m2 = dot(jnp.concatenate(sides(2), axis=1), wm[1])
    out_ref[2 * pair] = (dot(jnp.concatenate(sides(0) + own, axis=1), wy[0]) + (m1 + m2)).astype(BF)
    out_ref[2 * pair + 1] = (dot(jnp.concatenate(sides(3) + own, axis=1), wy[1]) + (m1 - m2)).astype(BF)


def partials(where, xv, inner_weight):
    rows, lon, channels = xv.shape
    depth, hidden = inner_weight.shape[1:]
    return pl.pallas_call(
        functools.partial(partial_kernel, rows // 2, lon),
        grid_spec=pltpu.PrefetchScalarGridSpec(
            num_scalar_prefetch=1,
            grid=(rows // 2,),
            in_specs=[
                held(),
                pl.BlockSpec(
                    (1, depth, hidden), lambda i, s: (s[0], 0, 0), pipeline_mode=pl.Buffered(1)
                ),
            ],
            out_specs=[held()] * 2,
            scratch_shapes=[
                pltpu.VMEM((2, 4 * channels, hidden), BF),
                pltpu.VMEM((2, 2 * channels, hidden), BF),
                pltpu.VMEM((4, lon + 16, channels), F32),
            ],
        ),
        out_shape=[
            pltpu.VMEM((rows, lon, hidden), BF),
            pltpu.VMEM((2, 3 * channels, hidden), BF),
        ],
        compiler_params=limits(28),
        cost_estimate=pl.CostEstimate(
            flops=rows * lon * 6 * channels * hidden * 2,
            bytes_accessed=rows * lon * (hidden + 2 * channels) * 2,
            transcendentals=0,
        ),
        name="own_rows",
    )(where, xv, inner_weight)


def finish_kernel(
    rows, lon, group, fluxes, where, table, weights, x_ref, part_ref, taps_ref, low_ref, high_ref, wl_ref,
    wm_ref, wh_ref, f_ref, o_ref, wet_ref, out_ref, halo, window, we, spread, wett, wetf,
):
    r = pl.program_id(0)
    parity = r % 2

    @pl.when(r == 0)
    def _():
        we[:, 0:384, :] = taps_ref[...]
        for e, side in enumerate((low_ref, high_ref)):
            v = side[...].astype(F32)
            halo[e, 8 : 8 + lon, :] = v
            halo[e, 7:8, :] = v[lon - 1 : lon]
            halo[e, 8 + lon : 9 + lon, :] = v[0:1]
        packs = [ref[...].astype(F32) for ref in (wl_ref, wm_ref, wh_ref)]
        for g in range(GROUPS):
            size = min(group, lon - g * group)
            owner = lane((group, 128)) // (rows * fluxes)
            total = jnp.zeros((group, 128), F32)
            for w, pack in enumerate(packs):
                shift = (rows * fluxes * (w - g)) % 128
                moved = pltpu.roll(pack, shift, 1) if shift else pack
                total = jnp.where(owner == w, moved, total)
            window[g * group : g * group + size, :] = total[0:size].astype(BF)
        at = sublane((128, spread.shape[1])) % fluxes
        total = jnp.zeros(spread.shape, F32)
        for f in range(fluxes):
            total = jnp.where(at == f, f_ref[0, f : f + 1, :].astype(F32) * 0.5, total)
        spread[...] = total
        wetf[...] = jnp.zeros_like(wetf)
        wetf[0:rows, 0:lon] = jnp.where(where[0] == 1, wet_ref[...].astype(F32), 1.0)
        for c in range(wetf.shape[1] // 128):
            wett[c * 128 : (c + 1) * 128, :] = wetf[:, c * 128 : (c + 1) * 128].T

    slot = sublane(spread.shape) // fluxes
    share = jnp.zeros(spread.shape, F32)
    row = where[1] * rows + r
    for m in range(table.shape[0]):
        local = table[m, where[0], row] - (where[1] - 1) * rows
        share += jnp.where(slot == local, weights[m, where[0], row], 0.0)
    we[parity, 384:512, :] = (share * spread[...]).astype(BF)

    def close(total):
        total = total + part_ref[r].astype(F32)
        act = (total + total * jnp.tanh(total)).astype(BF)
        value = x_ref[r].astype(F32) + dot(act, o_ref[0])
        keep = jnp.broadcast_to(wett[0:lon, 0:1], value.shape)
        out_ref[0] = jnp.where(keep > 0.5, value, 0.0).astype(BF)
        wett[...] = pltpu.roll(wett[...], 127, 1)

    edge = jnp.logical_or(r == 0, r == rows - 1)

    @pl.when(edge)
    def _():
        lhs = [halo[parity, k : k + lon, :].astype(BF) for k in (7, 9, 8)] + [window[...]]
        close(dot(jnp.concatenate(lhs, axis=1), we[parity]))

    @pl.when(jnp.logical_not(edge))
    def _():
        near = x_ref[jnp.clip(r - 1 + 2 * parity, 0, rows - 1)]
        close(dot(jnp.concatenate([near, window[...]], axis=1), we[parity, 256:512, :]))


def finish(where, xv, part, taps, beside, packs, forcing_in, outer_weight, wet_mask, table, weights):
    rows, lon, channels = xv.shape
    hidden = part.shape[2]
    fluxes = forcing_in.shape[1]
    group = packs[0].shape[0]
    scalars = pl.BlockSpec(memory_space=pltpu.SMEM)
    return pl.pallas_call(
        functools.partial(finish_kernel, rows, lon, group, fluxes),
        grid_spec=pltpu.PrefetchScalarGridSpec(
            num_scalar_prefetch=1,
            grid=(rows,),
            in_specs=[scalars, scalars] + [held()] * 8 + [
                pl.BlockSpec((1, fluxes, hidden), lambda r, s: (s[0], 0, 0)),
                pl.BlockSpec((1, hidden, channels), lambda r, s: (s[0], 0, 0)),
                pl.BlockSpec((rows, lon), lambda r, s: (s[1], 0)),
            ],
            out_specs=pl.BlockSpec((1, lon, channels), lambda r, s: (r, 0, 0)),
            scratch_shapes=[
                pltpu.VMEM((2, lon + 16, channels), F32),
                pltpu.VMEM((lon, 128), BF),
                pltpu.VMEM((2, 512, hidden), BF),
                pltpu.VMEM((128, hidden), F32),
                pltpu.VMEM((GROUPS * group, 128), F32),
                pltpu.VMEM((128, GROUPS * group), F32),
            ],
        ),
        out_shape=jax.ShapeDtypeStruct((rows, lon, channels), BF),
        compiler_params=limits(28),
        name="finish_rows",
    )(
        where, jnp.transpose(table, (2, 0, 1)), jnp.transpose(weights, (2, 0, 1)), xv, part, taps,
        *beside, *packs, forcing_in, outer_weight, wet_mask,
    )


def shards(state, inner_weight, outer_weight, surface_proj, forcing_in, margin_rows, margin_weights, wet_mask):
    count = lax.axis_size("lat")
    half = count // 2
    quarter = half // 2
    lon = state.shape[1]
    group = -(-lon // (GROUPS * 128)) * 128
    moved = (lax.axis_index("lat") + quarter) % count
    where = jnp.where(lax.iota(jnp.int32, 2) == 0, moved // half, moved % half)

    def component(i):
        return ((i + quarter) % count) // half

    def beside(block, distance):
        route = [(i, (i + distance) % count) for i in range(count)]
        route = [(i, j) for i, j in route if component(i) == component(j)]
        return lax.ppermute(block, "lat", route)

    pack, xv, up, down = surfaces(where, state, surface_proj, wet_mask, group)
    packs = []
    for offset in (1, 0, -1):
        route = [(i, (i + half + offset) % count) for i in range(count)]
        packs.append(lax.ppermute(pack, "lat", route))
    low = beside(up, 1)
    high = beside(down, -1)
    inner_weight, xv = lax.optimization_barrier((inner_weight, xv))
    part, taps = partials(where, xv, inner_weight)
    return finish(
        where, xv, part, taps, (low, high), packs, forcing_in, outer_weight, wet_mask, margin_rows, margin_weights
    )


def solution(mesh):
    placed = (P(("ens", "lat"), None, None), P(), P(), P(), P(), P(), P(), P())
    return jax.shard_map(
        shards, mesh=mesh, in_specs=placed, out_specs=P(("ens", "lat"), None, None), check_vma=False
    )
```

```python
import functools

import jax
import jax.numpy as jnp
from jax import lax
from jax.experimental import pallas as pl
from jax.experimental.pallas import tpu as pltpu
from jax.sharding import PartitionSpec as P

BF = jnp.bfloat16
F32 = jnp.float32
ACT = BF
GROUPS = 4


def dot(a, b):
    return jnp.dot(a, b, preferred_element_type=F32)


def lane(shape):
    return lax.broadcasted_iota(jnp.int32, shape, len(shape) - 1)


def sublane(shape):
    return lax.broadcasted_iota(jnp.int32, shape, len(shape) - 2)


def limits(mib):
    return pltpu.CompilerParams(
        dimension_semantics=("arbitrary",), vmem_limit_bytes=mib << 20
    )


def surface_kernel(
    rows, lon, group, fluxes, where, x_ref, proj_ref, wet_ref, out_ref, xv_ref, pair_ref, chip_ref, mask_ref,
    proj, wets, sems
):
    def load(k):
        both = pl.ds(2 * k, 2)
        copy = pltpu.make_async_copy(x_ref.at[both], xv_ref.at[both], sems.at[k])
        copy.start()
        return copy

    loads = [load(0)]
    small = [
        pltpu.make_async_copy(proj_ref.at[where[0]], proj, sems.at[rows // 2]),
        pltpu.make_async_copy(
            wet_ref.at[pl.ds(pl.multiple_of(where[1] * rows, rows), rows)], wets, sems.at[rows // 2 + 1]
        ),
    ]
    for copy in small:
        copy.start()
    loads.append(load(1))
    for copy in small:
        copy.wait()
    even = where[1] % 2 == 0
    channels = x_ref.shape[2]
    pick = (lane((rows, 128)) // fluxes == sublane((rows, 128))).astype(BF)
    wet = jnp.where(where[0] == 1, wets[...].astype(F32), 1.0).astype(BF)
    mask = lax.dot_general(wet, pick, (((0,), (0,)), ((), ())), preferred_element_type=F32)
    mask_ref[...] = mask.astype(BF)
    spread = (lane((fluxes, 128)) % fluxes == sublane((fluxes, 128))).astype(BF)
    tiled = lax.dot_general(
        proj[...], spread, (((0,), (0,)), ((), ())), preferred_element_type=F32
    ).astype(BF)
    owner = lane((channels, 128)) // fluxes
    total = None
    for k in range(rows // 2):
        halves = [jnp.where(owner == 2 * k + e, tiled, jnp.zeros_like(tiled)) for e in (0, 1)]
        loads[k].wait()
        if k + 2 < rows // 2:
            loads.append(load(k + 2))
        both = jnp.concatenate([xv_ref[2 * k], xv_ref[2 * k + 1]], axis=1)
        fields = dot(both, jnp.concatenate(halves, axis=0))
        total = fields if total is None else total + fields
    total = total * mask
    packed = jnp.zeros((group, 128), F32)
    for g in range(GROUPS):
        size = min(group, lon - g * group)
        part = total[g * group : g * group + size]
        if size < group:
            part = jnp.concatenate([part, jnp.zeros((group - size, 128), F32)], axis=0)
        packed += pltpu.roll(part, rows * fluxes * g, 1) if g else part
    packed = packed.astype(BF)
    out_ref[...] = packed
    pair_ref[0:lon, :] = xv_ref[jnp.where(even, rows - 1, 0)]
    pair_ref[lon : lon + group, :] = packed
    chip_ref[...] = xv_ref[jnp.where(even, 0, rows - 1)]


def in_hbm(x):
    return pltpu.with_memory_space_constraint(x, pltpu.HBM)


def held():
    return pl.BlockSpec(memory_space=pltpu.VMEM)


def surfaces(where, state, surface_proj, wet_mask, group):
    rows, lon, channels = state.shape
    fluxes = surface_proj.shape[2]
    return pl.pallas_call(
        functools.partial(surface_kernel, rows, lon, group, fluxes),
        grid_spec=pltpu.PrefetchScalarGridSpec(
            num_scalar_prefetch=1,
            grid=(1,),
            in_specs=[
                pl.BlockSpec(memory_space=pltpu.HBM),
                pl.BlockSpec(memory_space=pltpu.HBM),
                pl.BlockSpec(memory_space=pltpu.HBM),
            ],
            out_specs=[held()] * 5,
            scratch_shapes=[
                pltpu.VMEM((fluxes, channels), BF),
                pltpu.VMEM((rows, lon), jnp.int32),
                pltpu.SemaphoreType.DMA((rows // 2 + 2,)),
            ],
        ),
        out_shape=[
            pltpu.VMEM((group, 128), BF),
            pltpu.VMEM((rows, lon, channels), BF),
            pltpu.VMEM((lon + group, channels), BF),
            pltpu.VMEM((lon, channels), BF),
            pltpu.VMEM((lon, 128), BF),
        ],
        compiler_params=limits(16),
        name="surface_fields",
    )(
        where, in_hbm(state), in_hbm(jnp.swapaxes(surface_proj, 1, 2)), in_hbm(wet_mask)
    )


def partial_kernel(pairs, lon, where, x_ref, w_ref, out_ref, we, wy, wm, tf):
    def tap(a, b):
        return w_ref[0, (a * 3 + b) * 128 : (a * 3 + b + 1) * 128, :].astype(F32) * 0.5

    for k, (a, b) in enumerate(((0, 0), (0, 2), (1, 1), (2, 1))):
        wy[0, k * 128 : (k + 1) * 128, :] = tap(a, b).astype(BF)
    for k, (a, b) in enumerate(((2, 0), (2, 2), (0, 1), (1, 1))):
        wy[1, k * 128 : (k + 1) * 128, :] = tap(a, b).astype(BF)
    for k, b in enumerate((0, 2)):
        ends = tap(0, b) + tap(2, b)
        wm[0, k * 128 : (k + 1) * 128, :] = (0.5 * (ends + tap(1, b))).astype(BF)
        wm[1, k * 128 : (k + 1) * 128, :] = (0.5 * (ends - tap(1, b))).astype(BF)
    for e, a in enumerate((0, 2)):
        for k, b in enumerate((0, 2, 1)):
            we[e, k * 128 : (k + 1) * 128, :] = tap(a, b).astype(BF)

    for pair in range(pairs):
        slot = pair % tf.shape[0]
        own = [x_ref[2 * pair], x_ref[2 * pair + 1]]
        x1, x2 = own[0].astype(F32), own[1].astype(F32)
        low = x_ref[2 * pair - 1].astype(F32) - x2 if pair else -x2
        high = x_ref[2 * pair + 2].astype(F32) - x1 if pair < pairs - 1 else -x1
        for p, t in enumerate((low, x1 + x2, x2 - x1, high)):
            tf[slot, p, 8 : 8 + lon, :] = t
            tf[slot, p, 7:8, :] = t[lon - 1 : lon]
            tf[slot, p, 8 + lon : 9 + lon, :] = t[0:1]

        def sides(p):
            return [tf[slot, p, 7 : 7 + lon, :].astype(BF), tf[slot, p, 9 : 9 + lon, :].astype(BF)]

        m1 = dot(jnp.concatenate(sides(1), axis=1), wm[0])
        m2 = dot(jnp.concatenate(sides(2), axis=1), wm[1])
        out_ref[2 * pair] = (dot(jnp.concatenate(sides(0) + own, axis=1), wy[0]) + (m1 + m2)).astype(BF)
        out_ref[2 * pair + 1] = (dot(jnp.concatenate(sides(3) + own, axis=1), wy[1]) + (m1 - m2)).astype(BF)


def partials(where, xv, inner_weight):
    rows, lon, channels = xv.shape
    depth, hidden = inner_weight.shape[1:]
    return pl.pallas_call(
        functools.partial(partial_kernel, rows // 2, lon),
        grid_spec=pltpu.PrefetchScalarGridSpec(
            num_scalar_prefetch=1,
            grid=(1,),
            in_specs=[
                held(),
                pl.BlockSpec(
                    (1, depth, hidden), lambda i, s: (s[0], 0, 0), pipeline_mode=pl.Buffered(1)
                ),
            ],
            out_specs=[held()] * 2,
            scratch_shapes=[
                pltpu.VMEM((2, 4 * channels, hidden), BF),
                pltpu.VMEM((2, 2 * channels, hidden), BF),
                pltpu.VMEM((1, 4, lon + 16, channels), F32),
            ],
        ),
        out_shape=[
            pltpu.VMEM((rows, lon, hidden), BF),
            pltpu.VMEM((2, 3 * channels, hidden), BF),
        ],
        compiler_params=limits(34),
        cost_estimate=pl.CostEstimate(
            flops=rows * lon * 6 * channels * hidden * 2,
            bytes_accessed=rows * lon * (hidden + 2 * channels) * 2,
            transcendentals=0,
        ),
        name="own_rows",
    )(where, xv, inner_weight)


def finish_kernel(
    rows, lon, group, fluxes, where, table, weights, x_ref, part_ref, taps_ref, mask_ref, pair_ref, chip_ref,
    near_ref, far_ref, f_ref, o_ref, out_ref, halo, window, we, spread, done, sems,
):
    even = where[1] % 2 == 0
    swap = pair_ref[0:lon, :].astype(F32)
    chip = chip_ref[...].astype(F32)
    for e, v in enumerate((jnp.where(even, chip, swap), jnp.where(even, swap, chip))):
        halo[e, 8 : 8 + lon, :] = v
        halo[e, 7:8, :] = v[lon - 1 : lon]
        halo[e, 8 + lon : 9 + lon, :] = v[0:1]
    center = near_ref[0:group, :].astype(F32)
    other = near_ref[group : 2 * group, :].astype(F32)
    far = far_ref[...].astype(F32)
    packs = [jnp.where(even, far, other), center, jnp.where(even, other, far)]
    for g in range(GROUPS):
        size = min(group, lon - g * group)
        owner = lane((group, 128)) // (rows * fluxes)
        total = jnp.zeros((group, 128), F32)
        for w, pack in enumerate(packs):
            shift = (rows * fluxes * (w - g)) % 128
            moved = pltpu.roll(pack, shift, 1) if shift else pack
            total = jnp.where(owner == w, moved, total)
        window[g * group : g * group + size, :] = total[0:size].astype(BF)
    at = sublane((128, spread.shape[1])) % fluxes
    total = jnp.zeros(spread.shape, F32)
    for f in range(fluxes):
        total = jnp.where(at == f, f_ref[0, f : f + 1, :].astype(F32) * 0.5, total)
    spread[...] = total
    slot = sublane((128, 128)) // fluxes
    copies = []
    for r in range(rows):
        parity = r % 2
        edge = r in (0, rows - 1)
        share = jnp.zeros((128, 128), F32)
        row = where[1] * rows + r
        for m in range(table.shape[0]):
            local = table[m, where[0], row] - (where[1] - 1) * rows
            share += jnp.where(slot == local, weights[m, where[0], row], 0.0)
        share = jnp.concatenate([share] * (spread.shape[1] // 128), axis=1)
        base = 0 if edge else 256
        we[r, base:384, :] = taps_ref[parity, base:384, :]
        we[r, 384:512, :] = (share * spread[...]).astype(BF)
        if edge:
            lhs = [halo[parity, k : k + lon, :].astype(BF) for k in (7, 9, 8)]
        else:
            lhs = [x_ref[r + 1 if parity else r - 1]]
        total = dot(jnp.concatenate(lhs + [window[...]], axis=1), we[r, base:512, :])
        total = (total + part_ref[r].astype(F32)).astype(ACT)
        act = (total + total * jnp.tanh(total)).astype(BF)
        value = x_ref[r].astype(F32) + dot(act, o_ref[0])
        keep = jnp.broadcast_to(mask_ref[:, fluxes * r : fluxes * r + 1], value.shape)
        done[r] = value.astype(BF) * keep
        copy = pltpu.make_async_copy(done.at[r], out_ref.at[r], sems.at[r])
        copy.start()
        copies.append(copy)
    for copy in copies:
        copy.wait()


def finish(where, xv, part, taps, mask, received, forcing_in, outer_weight, table, weights):
    rows, lon, channels = xv.shape
    hidden = part.shape[2]
    fluxes = forcing_in.shape[1]
    group = received[3].shape[0]
    scalars = pl.BlockSpec(memory_space=pltpu.SMEM)
    return pl.pallas_call(
        functools.partial(finish_kernel, rows, lon, group, fluxes),
        grid_spec=pltpu.PrefetchScalarGridSpec(
            num_scalar_prefetch=1,
            grid=(1,),
            in_specs=[scalars, scalars] + [held()] * 8 + [
                pl.BlockSpec((1, fluxes, hidden), lambda r, s: (s[0], 0, 0)),
                pl.BlockSpec((1, hidden, channels), lambda r, s: (s[0], 0, 0)),
            ],
            out_specs=pl.BlockSpec(memory_space=pltpu.HBM),
            scratch_shapes=[
                pltpu.VMEM((2, lon + 16, channels), F32),
                pltpu.VMEM((lon, 128), BF),
                pltpu.VMEM((rows, 512, hidden), BF),
                pltpu.VMEM((128, hidden), F32),
                pltpu.VMEM((rows, lon, channels), BF),
                pltpu.SemaphoreType.DMA((rows,)),
            ],
        ),
        out_shape=jax.ShapeDtypeStruct((rows, lon, channels), BF),
        compiler_params=limits(34),
        name="finish_rows",
    )(
        where, jnp.transpose(table, (2, 0, 1)), jnp.transpose(weights, (2, 0, 1)), xv, part, taps, mask,
        *received, forcing_in, outer_weight,
    )


def shards(state, inner_weight, outer_weight, surface_proj, forcing_in, margin_rows, margin_weights, wet_mask):
    count = lax.axis_size("lat")
    half = count // 2
    quarter = half // 2
    lon = state.shape[1]
    group = -(-lon // (GROUPS * 128)) * 128
    moved = (lax.axis_index("lat") + quarter) % count
    where = jnp.where(lax.iota(jnp.int32, 2) == 0, moved // half, moved % half)

    def component(i):
        return ((i + quarter) % count) // half

    def send(block, target):
        return lax.ppermute(block, "lat", [(i, target(i) % count) for i in range(count)])

    pack, xv, pair, chip, mask = surfaces(where, state, surface_proj, wet_mask, group)
    pair = send(pair, lambda i: i + 1 - 2 * (i % 2))
    links = [(i, (i + (1 if i % 2 else -1)) % count) for i in range(count)]
    chip = lax.ppermute(chip, "lat", [(i, j) for i, j in links if component(i) == component(j)])
    far = send(pack, lambda i: i + half + (1 if i % 2 else -1))
    near = send(jnp.concatenate([pack, pair[lon:]], axis=0), lambda i: i + half)
    part, taps = partials(where, xv, inner_weight)
    return finish(
        where, xv, part, taps, mask, (pair, chip, near, far), forcing_in, outer_weight, margin_rows, margin_weights
    )


def solution(mesh):
    placed = (P(("ens", "lat"), None, None), P(), P(), P(), P(), P(), P(), P())
    return jax.shard_map(
        shards, mesh=mesh, in_specs=placed, out_specs=P(("ens", "lat"), None, None), check_vma=False
    )
```

```python
import functools

import jax
import jax.numpy as jnp
from jax import lax
from jax.experimental import pallas as pl
from jax.experimental.pallas import tpu as pltpu
from jax.sharding import PartitionSpec as P

BF = jnp.bfloat16
F32 = jnp.float32
ACT = BF
GROUPS = 4


def dot(a, b):
    return jnp.dot(a, b, preferred_element_type=F32)


def lane(shape):
    return lax.broadcasted_iota(jnp.int32, shape, len(shape) - 1)


def sublane(shape):
    return lax.broadcasted_iota(jnp.int32, shape, len(shape) - 2)


def limits(mib):
    return pltpu.CompilerParams(
        dimension_semantics=("arbitrary",), vmem_limit_bytes=mib << 20
    )


def surface_kernel(
    rows, lon, group, fluxes, where, x_ref, proj_ref, wet_ref, out_ref, xv_ref, pair_ref, chip_ref, mask_ref,
    proj, wets, sems
):
    def load(k):
        both = pl.ds(2 * k, 2)
        copy = pltpu.make_async_copy(x_ref.at[both], xv_ref.at[both], sems.at[k])
        copy.start()
        return copy

    loads = [load(0)]
    small = [
        pltpu.make_async_copy(proj_ref.at[where[0]], proj, sems.at[rows // 2]),
        pltpu.make_async_copy(
            wet_ref.at[pl.ds(pl.multiple_of(where[1] * rows, rows), rows)], wets, sems.at[rows // 2 + 1]
        ),
    ]
    for copy in small:
        copy.start()
    loads.append(load(1))
    for copy in small:
        copy.wait()
    even = where[1] % 2 == 0
    channels = x_ref.shape[2]
    pick = (lane((rows, 128)) // fluxes == sublane((rows, 128))).astype(BF)
    wet = jnp.where(where[0] == 1, wets[...].astype(F32), 1.0).astype(BF)
    mask = lax.dot_general(wet, pick, (((0,), (0,)), ((), ())), preferred_element_type=F32)
    mask_ref[...] = mask.astype(BF)
    spread = (lane((fluxes, 128)) % fluxes == sublane((fluxes, 128))).astype(BF)
    tiled = lax.dot_general(
        proj[...], spread, (((0,), (0,)), ((), ())), preferred_element_type=F32
    ).astype(BF)
    owner = lane((channels, 128)) // fluxes
    total = None
    for k in range(rows // 2):
        halves = [jnp.where(owner == 2 * k + e, tiled, jnp.zeros_like(tiled)) for e in (0, 1)]
        loads[k].wait()
        if k + 2 < rows // 2:
            loads.append(load(k + 2))
        both = jnp.concatenate([xv_ref[2 * k], xv_ref[2 * k + 1]], axis=1)
        mixed = jnp.concatenate(halves, axis=0)
        fields = jnp.concatenate([dot(both[: lon // 2], mixed), dot(both[lon // 2 :], mixed)], axis=0)
        total = fields if total is None else total + fields
    total = total * mask
    packed = jnp.zeros((group, 128), F32)
    for g in range(GROUPS):
        size = min(group, lon - g * group)
        part = total[g * group : g * group + size]
        if size < group:
            part = jnp.concatenate([part, jnp.zeros((group - size, 128), F32)], axis=0)
        packed += pltpu.roll(part, rows * fluxes * g, 1) if g else part
    packed = packed.astype(BF)
    out_ref[...] = packed
    pair_ref[0:lon, :] = xv_ref[jnp.where(even, rows - 1, 0)]
    pair_ref[lon : lon + group, :] = packed
    chip_ref[...] = xv_ref[jnp.where(even, 0, rows - 1)]


def in_hbm(x):
    return pltpu.with_memory_space_constraint(x, pltpu.HBM)


def held():
    return pl.BlockSpec(memory_space=pltpu.VMEM)


def surfaces(where, state, surface_proj, wet_mask, group):
    rows, lon, channels = state.shape
    fluxes = surface_proj.shape[2]
    return pl.pallas_call(
        functools.partial(surface_kernel, rows, lon, group, fluxes),
        grid_spec=pltpu.PrefetchScalarGridSpec(
            num_scalar_prefetch=1,
            grid=(1,),
            in_specs=[
                pl.BlockSpec(memory_space=pltpu.HBM),
                pl.BlockSpec(memory_space=pltpu.HBM),
                pl.BlockSpec(memory_space=pltpu.HBM),
            ],
            out_specs=[held()] * 5,
            scratch_shapes=[
                pltpu.VMEM((fluxes, channels), BF),
                pltpu.VMEM((rows, lon), jnp.int32),
                pltpu.SemaphoreType.DMA((rows // 2 + 2,)),
            ],
        ),
        out_shape=[
            pltpu.VMEM((group, 128), BF),
            pltpu.VMEM((rows, lon, channels), BF),
            pltpu.VMEM((lon + group, channels), BF),
            pltpu.VMEM((lon, channels), BF),
            pltpu.VMEM((lon, 128), BF),
        ],
        compiler_params=limits(16),
        name="surface_fields",
    )(
        where, in_hbm(state), in_hbm(jnp.swapaxes(surface_proj, 1, 2)), in_hbm(wet_mask)
    )


def partial_kernel(pairs, lon, fluxes, where, table, weights, x_ref, w_ref, f_ref, out_ref, we, wy, wm, tf):
    def tap(a, b):
        return w_ref[0, (a * 3 + b) * 128 : (a * 3 + b + 1) * 128, :].astype(F32) * 0.5

    for k, (a, b) in enumerate(((0, 0), (0, 2), (1, 1), (2, 1))):
        wy[0, k * 128 : (k + 1) * 128, :] = tap(a, b).astype(BF)
    for k, (a, b) in enumerate(((2, 0), (2, 2), (0, 1), (1, 1))):
        wy[1, k * 128 : (k + 1) * 128, :] = tap(a, b).astype(BF)
    for k, b in enumerate((0, 2)):
        ends = tap(0, b) + tap(2, b)
        wm[0, k * 128 : (k + 1) * 128, :] = (0.5 * (ends + tap(1, b))).astype(BF)
        wm[1, k * 128 : (k + 1) * 128, :] = (0.5 * (ends - tap(1, b))).astype(BF)
    rows = 2 * pairs
    hidden = f_ref.shape[2]
    at = sublane((128, hidden)) % fluxes
    spread = jnp.zeros((128, hidden), F32)
    for f in range(fluxes):
        spread = jnp.where(at == f, f_ref[0, f : f + 1, :].astype(F32) * 0.5, spread)

    def finishing_weights(r):
        for k, b in enumerate((0, 2, 1)):
            if k == 2 or r in (0, rows - 1):
                we[r, k * 128 : (k + 1) * 128, :] = tap(2 * (r % 2), b).astype(BF)
        share = jnp.zeros((128, 128), F32)
        row = where[1] * rows + r
        for m in range(table.shape[0]):
            local = table[m, where[0], row] - (where[1] - 1) * rows
            share += jnp.where(sublane((128, 128)) // fluxes == local, weights[m, where[0], row], 0.0)
        share = jnp.concatenate([share] * (hidden // 128), axis=1)
        we[r, 384:512, :] = (share * spread).astype(BF)

    for pair in range(pairs):
        slot = pair % tf.shape[0]
        own = [x_ref[2 * pair], x_ref[2 * pair + 1]]
        x1, x2 = own[0].astype(F32), own[1].astype(F32)
        low = x_ref[2 * pair - 1].astype(F32) - x2 if pair else -x2
        high = x_ref[2 * pair + 2].astype(F32) - x1 if pair < pairs - 1 else -x1
        for p, t in enumerate((low, x1 + x2, x2 - x1, high)):
            tf[slot, p, 8 : 8 + lon, :] = t
            tf[slot, p, 7:8, :] = t[lon - 1 : lon]
            tf[slot, p, 8 + lon : 9 + lon, :] = t[0:1]

        def sides(p):
            return [tf[slot, p, 7 : 7 + lon, :].astype(BF), tf[slot, p, 9 : 9 + lon, :].astype(BF)]

        m1 = dot(jnp.concatenate(sides(1), axis=1), wm[0])
        m2 = dot(jnp.concatenate(sides(2), axis=1), wm[1])
        out_ref[2 * pair] = (dot(jnp.concatenate(sides(0) + own, axis=1), wy[0]) + (m1 + m2)).astype(BF)
        finishing_weights(2 * pair)
        finishing_weights(2 * pair + 1)
        out_ref[2 * pair + 1] = (dot(jnp.concatenate(sides(3) + own, axis=1), wy[1]) + (m1 - m2)).astype(BF)


def partials(where, xv, inner_weight, forcing_in, table, weights):
    rows, lon, channels = xv.shape
    depth, hidden = inner_weight.shape[1:]
    fluxes = forcing_in.shape[1]
    scalars = pl.BlockSpec(memory_space=pltpu.SMEM)
    return pl.pallas_call(
        functools.partial(partial_kernel, rows // 2, lon, fluxes),
        grid_spec=pltpu.PrefetchScalarGridSpec(
            num_scalar_prefetch=1,
            grid=(1,),
            in_specs=[
                scalars,
                scalars,
                held(),
                pl.BlockSpec(
                    (1, depth, hidden), lambda i, s: (s[0], 0, 0), pipeline_mode=pl.Buffered(1)
                ),
                pl.BlockSpec((1, fluxes, hidden), lambda i, s: (s[0], 0, 0)),
            ],
            out_specs=[held()] * 2,
            scratch_shapes=[
                pltpu.VMEM((2, 4 * channels, hidden), BF),
                pltpu.VMEM((2, 2 * channels, hidden), BF),
                pltpu.VMEM((1, 4, lon + 16, channels), F32),
            ],
        ),
        out_shape=[
            pltpu.VMEM((rows, lon, hidden), BF),
            pltpu.VMEM((rows, 4 * channels, hidden), BF),
        ],
        compiler_params=limits(24),
        cost_estimate=pl.CostEstimate(
            flops=rows * lon * 6 * channels * hidden * 2,
            bytes_accessed=rows * lon * (hidden + 2 * channels) * 2,
            transcendentals=0,
        ),
        name="own_rows",
    )(
        where, jnp.transpose(table, (2, 0, 1)), jnp.transpose(weights, (2, 0, 1)), xv, inner_weight, forcing_in
    )


def finish_kernel(
    rows, lon, group, fluxes, where, x_ref, part_ref, we, mask_ref, pair_ref, chip_ref, near_ref, far_ref,
    o_ref, out_ref, halo, window, done, sems,
):
    even = where[1] % 2 == 0
    center = near_ref[0:group, :].astype(F32)
    other = near_ref[group : 2 * group, :].astype(F32)
    far = far_ref[...].astype(F32)
    packs = [jnp.where(even, far, other), center, jnp.where(even, other, far)]
    for g in range(GROUPS):
        size = min(group, lon - g * group)
        owner = lane((group, 128)) // (rows * fluxes)
        total = jnp.zeros((group, 128), F32)
        for w, pack in enumerate(packs):
            shift = (rows * fluxes * (w - g)) % 128
            moved = pltpu.roll(pack, shift, 1) if shift else pack
            total = jnp.where(owner == w, moved, total)
        window[g * group : g * group + size, :] = total[0:size].astype(BF)
    copies = []
    for r in list(range(1, rows - 1)) + [0, rows - 1]:
        parity = r % 2
        edge = r in (0, rows - 1)
        base = 0 if edge else 256
        if r == 0:
            swap = pair_ref[0:lon, :].astype(F32)
            chip = chip_ref[...].astype(F32)
            for e, v in enumerate((jnp.where(even, chip, swap), jnp.where(even, swap, chip))):
                halo[e, 8 : 8 + lon, :] = v
                halo[e, 7:8, :] = v[lon - 1 : lon]
                halo[e, 8 + lon : 9 + lon, :] = v[0:1]
        if edge:
            lhs = [halo[parity, k : k + lon, :].astype(BF) for k in (7, 9, 8)]
        else:
            lhs = [x_ref[r + 1 if parity else r - 1]]
        total = dot(jnp.concatenate(lhs + [window[...]], axis=1), we[r, base:512, :])
        total = (total + part_ref[r].astype(F32)).astype(ACT)
        act = (total + total * jnp.tanh(total)).astype(BF)
        value = x_ref[r].astype(F32) + dot(act, o_ref[0])
        keep = jnp.broadcast_to(mask_ref[:, fluxes * r : fluxes * r + 1], value.shape)
        done[r] = value.astype(BF) * keep
        copy = pltpu.make_async_copy(done.at[r], out_ref.at[r], sems.at[r])
        copy.start()
        copies.append(copy)
    for copy in copies:
        copy.wait()


def finish(where, xv, part, taps, mask, received, outer_weight, fluxes):
    rows, lon, channels = xv.shape
    hidden = part.shape[2]
    group = received[3].shape[0]
    return pl.pallas_call(
        functools.partial(finish_kernel, rows, lon, group, fluxes),
        grid_spec=pltpu.PrefetchScalarGridSpec(
            num_scalar_prefetch=1,
            grid=(1,),
            in_specs=[held()] * 8 + [
                pl.BlockSpec((1, hidden, channels), lambda r, s: (s[0], 0, 0)),
            ],
            out_specs=pl.BlockSpec(memory_space=pltpu.HBM),
            scratch_shapes=[
                pltpu.VMEM((2, lon + 16, channels), F32),
                pltpu.VMEM((lon, 128), BF),
                pltpu.VMEM((rows, lon, channels), BF),
                pltpu.SemaphoreType.DMA((rows,)),
            ],
        ),
        out_shape=jax.ShapeDtypeStruct((rows, lon, channels), BF),
        compiler_params=limits(20),
        name="finish_rows",
    )(
        where, xv, part, taps, mask, *received, outer_weight
    )


def shards(state, inner_weight, outer_weight, surface_proj, forcing_in, margin_rows, margin_weights, wet_mask):
    count = lax.axis_size("lat")
    half = count // 2
    quarter = half // 2
    lon = state.shape[1]
    group = -(-lon // (GROUPS * 128)) * 128
    moved = (lax.axis_index("lat") + quarter) % count
    where = jnp.where(lax.iota(jnp.int32, 2) == 0, moved // half, moved % half)

    def component(i):
        return ((i + quarter) % count) // half

    def send(block, target):
        return lax.ppermute(block, "lat", [(i, target(i) % count) for i in range(count)])

    pack, xv, pair, chip, mask = surfaces(where, state, surface_proj, wet_mask, group)
    pair = send(pair, lambda i: i + 1 - 2 * (i % 2))
    links = [(i, (i + (1 if i % 2 else -1)) % count) for i in range(count)]
    far = send(pack, lambda i: i + half + (1 if i % 2 else -1))
    near = jnp.concatenate([pack, pair[lon:]], axis=0)
    near, chip = lax.optimization_barrier((near, chip))
    near = send(near, lambda i: i + half)
    chip = lax.ppermute(chip, "lat", [(i, j) for i, j in links if component(i) == component(j)])
    part, taps = partials(where, xv, inner_weight, forcing_in, margin_rows, margin_weights)
    return finish(
        where, xv, part, taps, mask, (pair, chip, near, far), outer_weight, forcing_in.shape[1]
    )


def solution(mesh):
    placed = (P(("ens", "lat"), None, None), P(), P(), P(), P(), P(), P(), P())
    return jax.shard_map(
        shards, mesh=mesh, in_specs=placed, out_specs=P(("ens", "lat"), None, None), check_vma=False
    )
```

```python
import functools

import jax
import jax.numpy as jnp
from jax import lax
from jax.experimental import pallas as pl
from jax.experimental.pallas import tpu as pltpu
from jax.sharding import PartitionSpec as P

BF = jnp.bfloat16
F32 = jnp.float32
ACT = BF
GROUPS = 4


def dot(a, b):
    return jnp.dot(a, b, preferred_element_type=F32)


def lane(shape):
    return lax.broadcasted_iota(jnp.int32, shape, len(shape) - 1)


def sublane(shape):
    return lax.broadcasted_iota(jnp.int32, shape, len(shape) - 2)


def limits(mib):
    return pltpu.CompilerParams(
        dimension_semantics=("arbitrary",), vmem_limit_bytes=mib << 20
    )


def surface_kernel(
    rows, lon, group, fluxes, where, x_ref, proj_ref, wet_ref, f_ref, table_ref, margin_ref, w_ref, out_ref,
    xv_ref, pair_ref, chip_ref, mask_ref, force_ref, wv_ref, proj, wets, fmap, table, margin, sems,
):
    def load(k):
        both = pl.ds(2 * k, 2)
        copy = pltpu.make_async_copy(x_ref.at[both], xv_ref.at[both], sems.at[k])
        copy.start()
        return copy

    loads = [load(0)]
    small = [
        pltpu.make_async_copy(proj_ref.at[where[0]], proj, sems.at[rows // 2]),
        pltpu.make_async_copy(
            wet_ref.at[pl.ds(pl.multiple_of(where[1] * rows, rows), rows)], wets, sems.at[rows // 2 + 1]
        ),
        pltpu.make_async_copy(f_ref.at[where[0]], fmap, sems.at[rows // 2 + 2]),
        pltpu.make_async_copy(table_ref, table, sems.at[rows // 2 + 3]),
        pltpu.make_async_copy(margin_ref, margin, sems.at[rows // 2 + 4]),
    ]
    for copy in small:
        copy.start()
    loads += [load(k) for k in range(1, rows // 2)]
    for copy in small:
        copy.wait()
    hidden = fmap.shape[1]
    at = sublane((128, hidden)) % fluxes
    spread = jnp.zeros((128, hidden), F32)
    for f in range(fluxes):
        spread = jnp.where(at == f, fmap[f : f + 1, :].astype(F32) * 0.5, spread)
    for r in range(rows):
        share = jnp.zeros((128, 128), F32)
        row = where[1] * rows + r
        for m in range(table.shape[0]):
            local = table[m, where[0], row] - (where[1] - 1) * rows
            share += jnp.where(sublane((128, 128)) // fluxes == local, margin[m, where[0], row], 0.0)
        share = jnp.concatenate([share] * (hidden // 128), axis=1)
        force_ref[r] = (share * spread).astype(BF)
    even = where[1] % 2 == 0
    channels = x_ref.shape[2]
    pick = (lane((rows, 128)) // fluxes == sublane((rows, 128))).astype(BF)
    wet = jnp.where(where[0] == 1, wets[...].astype(F32), 1.0).astype(BF)
    mask = lax.dot_general(wet, pick, (((0,), (0,)), ((), ())), preferred_element_type=F32)
    mask_ref[...] = mask.astype(BF)
    spread = (lane((fluxes, 128)) % fluxes == sublane((fluxes, 128))).astype(BF)
    tiled = lax.dot_general(
        proj[...], spread, (((0,), (0,)), ((), ())), preferred_element_type=F32
    ).astype(BF)
    owner = lane((channels, 128)) // fluxes
    total = None
    for k in range(rows // 2):
        halves = [jnp.where(owner == 2 * k + e, tiled, jnp.zeros_like(tiled)) for e in (0, 1)]
        loads[k].wait()
        if k == 0:
            inner = pltpu.make_async_copy(w_ref.at[where[0]], wv_ref, sems.at[rows // 2 + 5])
            inner.start()
        both = jnp.concatenate([xv_ref[2 * k], xv_ref[2 * k + 1]], axis=1)
        mixed = jnp.concatenate(halves, axis=0)
        fields = jnp.concatenate([dot(both[: lon // 2], mixed), dot(both[lon // 2 :], mixed)], axis=0)
        total = fields if total is None else total + fields
    total = total * mask
    packed = jnp.zeros((group, 128), F32)
    for g in range(GROUPS):
        size = min(group, lon - g * group)
        part = total[g * group : g * group + size]
        if size < group:
            part = jnp.concatenate([part, jnp.zeros((group - size, 128), F32)], axis=0)
        packed += pltpu.roll(part, rows * fluxes * g, 1) if g else part
    packed = packed.astype(BF)
    out_ref[...] = packed
    pair_ref[0:lon, :] = xv_ref[jnp.where(even, rows - 1, 0)]
    pair_ref[lon : lon + group, :] = packed
    chip_ref[...] = xv_ref[jnp.where(even, 0, rows - 1)]
    inner.wait()


def in_hbm(x):
    return pltpu.with_memory_space_constraint(x, pltpu.HBM)


def held():
    return pl.BlockSpec(memory_space=pltpu.VMEM)


def surfaces(where, state, surface_proj, wet_mask, forcing_in, table, weights, inner_weight, group):
    depth, hidden = inner_weight.shape[1:]
    rows, lon, channels = state.shape
    fluxes = surface_proj.shape[2]
    return pl.pallas_call(
        functools.partial(surface_kernel, rows, lon, group, fluxes),
        grid_spec=pltpu.PrefetchScalarGridSpec(
            num_scalar_prefetch=1,
            grid=(1,),
            in_specs=[pl.BlockSpec(memory_space=pltpu.HBM)] * 7,
            out_specs=[held()] * 7,
            scratch_shapes=[
                pltpu.VMEM((fluxes, channels), BF),
                pltpu.VMEM((rows, lon), jnp.int32),
                pltpu.VMEM((fluxes, hidden), BF),
                pltpu.SMEM(table.shape, jnp.int32),
                pltpu.SMEM(table.shape, F32),
                pltpu.SemaphoreType.DMA((rows // 2 + 6,)),
            ],
        ),
        out_shape=[
            pltpu.VMEM((group, 128), BF),
            pltpu.VMEM((rows, lon, channels), BF),
            pltpu.VMEM((lon + group, channels), BF),
            pltpu.VMEM((lon, channels), BF),
            pltpu.VMEM((lon, 128), BF),
            pltpu.VMEM((rows, 128, hidden), BF),
            pltpu.VMEM((depth, hidden), BF),
        ],
        compiler_params=limits(16),
        name="surface_fields",
    )(
        where,
        *[
            in_hbm(x)
            for x in (
                state, jnp.swapaxes(surface_proj, 1, 2), wet_mask, forcing_in, table, weights, inner_weight
            )
        ],
    )


def partial_kernel(pairs, lon, x_ref, w_ref, out_ref, we, wy, wm, tf):
    def tap(a, b):
        return w_ref[(a * 3 + b) * 128 : (a * 3 + b + 1) * 128, :].astype(F32) * 0.5

    for k, (a, b) in enumerate(((0, 0), (0, 2), (1, 1), (2, 1))):
        wy[0, k * 128 : (k + 1) * 128, :] = tap(a, b).astype(BF)
    for k, (a, b) in enumerate(((2, 0), (2, 2), (0, 1), (1, 1))):
        wy[1, k * 128 : (k + 1) * 128, :] = tap(a, b).astype(BF)
    for k, b in enumerate((0, 2)):
        ends = tap(0, b) + tap(2, b)
        wm[0, k * 128 : (k + 1) * 128, :] = (0.5 * (ends + tap(1, b))).astype(BF)
        wm[1, k * 128 : (k + 1) * 128, :] = (0.5 * (ends - tap(1, b))).astype(BF)
    for e, a in enumerate((0, 2)):
        for k, b in enumerate((0, 2, 1)):
            we[e, k * 128 : (k + 1) * 128, :] = tap(a, b).astype(BF)

    for pair in range(pairs):
        slot = pair % tf.shape[0]
        own = [x_ref[2 * pair], x_ref[2 * pair + 1]]
        x1, x2 = own[0].astype(F32), own[1].astype(F32)
        low = x_ref[2 * pair - 1].astype(F32) - x2 if pair else -x2
        high = x_ref[2 * pair + 2].astype(F32) - x1 if pair < pairs - 1 else -x1
        for p, t in enumerate((low, x1 + x2, x2 - x1, high)):
            tf[slot, p, 8 : 8 + lon, :] = t
            tf[slot, p, 7:8, :] = t[lon - 1 : lon]
            tf[slot, p, 8 + lon : 9 + lon, :] = t[0:1]

        def sides(p):
            return [tf[slot, p, 7 : 7 + lon, :].astype(BF), tf[slot, p, 9 : 9 + lon, :].astype(BF)]

        m1 = dot(jnp.concatenate(sides(1), axis=1), wm[0])
        m2 = dot(jnp.concatenate(sides(2), axis=1), wm[1])
        out_ref[2 * pair] = (dot(jnp.concatenate(sides(0) + own, axis=1), wy[0]) + (m1 + m2)).astype(BF)
        out_ref[2 * pair + 1] = (dot(jnp.concatenate(sides(3) + own, axis=1), wy[1]) + (m1 - m2)).astype(BF)


def partials(xv, inner):
    rows, lon, channels = xv.shape
    hidden = inner.shape[1]
    return pl.pallas_call(
        functools.partial(partial_kernel, rows // 2, lon),
        in_specs=[held()] * 2,
        out_specs=[held()] * 2,
        scratch_shapes=[
            pltpu.VMEM((2, 4 * channels, hidden), BF),
            pltpu.VMEM((2, 2 * channels, hidden), BF),
            pltpu.VMEM((1, 4, lon + 16, channels), F32),
        ],
        out_shape=[
            pltpu.VMEM((rows, lon, hidden), BF),
            pltpu.VMEM((2, 3 * channels, hidden), BF),
        ],
        compiler_params=pltpu.CompilerParams(vmem_limit_bytes=26 << 20),
        cost_estimate=pl.CostEstimate(
            flops=rows * lon * 6 * channels * hidden * 2,
            bytes_accessed=rows * lon * (hidden + 2 * channels) * 2,
            transcendentals=0,
        ),
        name="own_rows",
    )(xv, inner)


def finish_kernel(
    rows, lon, group, fluxes, where, x_ref, part_ref, taps_ref, force_ref, mask_ref, pair_ref, chip_ref, near_ref, far_ref,
    o_ref, out_ref, halo, window, done, sems,
):
    even = where[1] % 2 == 0
    center = near_ref[0:group, :].astype(F32)
    other = near_ref[group : 2 * group, :].astype(F32)
    far = far_ref[...].astype(F32)
    packs = [jnp.where(even, far, other), center, jnp.where(even, other, far)]
    for g in range(GROUPS):
        size = min(group, lon - g * group)
        owner = lane((group, 128)) // (rows * fluxes)
        total = jnp.zeros((group, 128), F32)
        for w, pack in enumerate(packs):
            shift = (rows * fluxes * (w - g)) % 128
            moved = pltpu.roll(pack, shift, 1) if shift else pack
            total = jnp.where(owner == w, moved, total)
        window[g * group : g * group + size, :] = total[0:size].astype(BF)
    copies = []
    for r in list(range(1, rows - 1)) + [0, rows - 1]:
        parity = r % 2
        edge = r in (0, rows - 1)
        base = 0 if edge else 256
        if r == 0:
            swap = pair_ref[0:lon, :].astype(F32)
            chip = chip_ref[...].astype(F32)
            for e, v in enumerate((jnp.where(even, chip, swap), jnp.where(even, swap, chip))):
                halo[e, 8 : 8 + lon, :] = v
                halo[e, 7:8, :] = v[lon - 1 : lon]
                halo[e, 8 + lon : 9 + lon, :] = v[0:1]
        if edge:
            lhs = [halo[parity, k : k + lon, :].astype(BF) for k in (7, 9, 8)]
        else:
            lhs = [x_ref[r + 1 if parity else r - 1]]
        total = dot(jnp.concatenate(lhs + [window[...]], axis=1), jnp.concatenate([taps_ref[parity, base:, :], force_ref[r]], axis=0))
        total = (total + part_ref[r].astype(F32)).astype(ACT)
        act = (total + total * jnp.tanh(total)).astype(BF)
        value = x_ref[r].astype(F32) + dot(act, o_ref[0])
        keep = jnp.broadcast_to(mask_ref[:, fluxes * r : fluxes * r + 1], value.shape)
        done[r] = value.astype(BF) * keep
        copy = pltpu.make_async_copy(done.at[r], out_ref.at[r], sems.at[r])
        copy.start()
        copies.append(copy)
    for copy in copies:
        copy.wait()


def finish(where, xv, part, taps, force, mask, received, outer_weight, fluxes):
    rows, lon, channels = xv.shape
    hidden = part.shape[2]
    group = received[3].shape[0]
    return pl.pallas_call(
        functools.partial(finish_kernel, rows, lon, group, fluxes),
        grid_spec=pltpu.PrefetchScalarGridSpec(
            num_scalar_prefetch=1,
            grid=(1,),
            in_specs=[held()] * 9 + [
                pl.BlockSpec((1, hidden, channels), lambda r, s: (s[0], 0, 0)),
            ],
            out_specs=pl.BlockSpec(memory_space=pltpu.HBM),
            scratch_shapes=[
                pltpu.VMEM((2, lon + 16, channels), F32),
                pltpu.VMEM((lon, 128), BF),
                pltpu.VMEM((rows, lon, channels), BF),
                pltpu.SemaphoreType.DMA((rows,)),
            ],
        ),
        out_shape=jax.ShapeDtypeStruct((rows, lon, channels), BF),
        compiler_params=limits(20),
        name="finish_rows",
    )(
        where, xv, part, taps, force, mask, *received, outer_weight
    )


def shards(state, inner_weight, outer_weight, surface_proj, forcing_in, margin_rows, margin_weights, wet_mask):
    count = lax.axis_size("lat")
    half = count // 2
    quarter = half // 2
    lon = state.shape[1]
    group = -(-lon // (GROUPS * 128)) * 128
    moved = (lax.axis_index("lat") + quarter) % count
    where = jnp.where(lax.iota(jnp.int32, 2) == 0, moved // half, moved % half)

    def component(i):
        return ((i + quarter) % count) // half

    def send(block, target):
        return lax.ppermute(block, "lat", [(i, target(i) % count) for i in range(count)])

    pack, xv, pair, chip, mask, force, inner = surfaces(
        where, state, surface_proj, wet_mask, forcing_in, jnp.transpose(margin_rows, (2, 0, 1)),
        jnp.transpose(margin_weights, (2, 0, 1)), inner_weight, group,
    )
    pair = send(pair, lambda i: i + 1 - 2 * (i % 2))
    links = [(i, (i + (1 if i % 2 else -1)) % count) for i in range(count)]
    far = send(pack, lambda i: i + half + (1 if i % 2 else -1))
    near = jnp.concatenate([pack, pair[lon:]], axis=0)
    near, chip = lax.optimization_barrier((near, chip))
    near = send(near, lambda i: i + half)
    chip = lax.ppermute(chip, "lat", [(i, j) for i, j in links if component(i) == component(j)])
    part, taps = partials(xv, inner)
    return finish(where, xv, part, taps, force, mask, (pair, chip, near, far), outer_weight, forcing_in.shape[1])


def solution(mesh):
    placed = (P(("ens", "lat"), None, None), P(), P(), P(), P(), P(), P(), P())
    return jax.shard_map(
        shards, mesh=mesh, in_specs=placed, out_specs=P(("ens", "lat"), None, None), check_vma=False
    )
```

```python
import functools

import jax
import jax.numpy as jnp
from jax import lax
from jax.experimental import pallas as pl
from jax.experimental.pallas import tpu as pltpu
from jax.sharding import PartitionSpec as P

BF = jnp.bfloat16
F32 = jnp.float32
ACT = BF
GROUPS = 4


def dot(a, b):
    return jnp.dot(a, b, preferred_element_type=F32)


def lane(shape):
    return lax.broadcasted_iota(jnp.int32, shape, len(shape) - 1)


def sublane(shape):
    return lax.broadcasted_iota(jnp.int32, shape, len(shape) - 2)


def limits(mib):
    return pltpu.CompilerParams(
        dimension_semantics=("arbitrary",), vmem_limit_bytes=mib << 20
    )


def surface_kernel(
    rows, lon, group, fluxes, where, x_ref, proj_ref, wet_ref, f_ref, table_ref, margin_ref, w_ref, out_ref,
    xv_ref, pair_ref, chip_ref, mask_ref, force_ref, wv_ref, proj, wets, fmap, table, margin, sems,
):
    def load(k):
        both = pl.ds(2 * k, 2)
        copy = pltpu.make_async_copy(x_ref.at[both], xv_ref.at[both], sems.at[k])
        copy.start()
        return copy

    loads = [load(0)]
    small = [
        pltpu.make_async_copy(proj_ref.at[where[0]], proj, sems.at[rows // 2]),
        pltpu.make_async_copy(
            wet_ref.at[pl.ds(pl.multiple_of(where[1] * rows, rows), rows)], wets, sems.at[rows // 2 + 1]
        ),
        pltpu.make_async_copy(f_ref.at[where[0]], fmap, sems.at[rows // 2 + 2]),
        pltpu.make_async_copy(table_ref, table, sems.at[rows // 2 + 3]),
        pltpu.make_async_copy(margin_ref, margin, sems.at[rows // 2 + 4]),
    ]
    for copy in small:
        copy.start()
    loads += [load(k) for k in range(1, rows // 2)]
    for copy in small:
        copy.wait()
    hidden = fmap.shape[1]
    at = sublane((128, hidden)) % fluxes
    spread = jnp.zeros((128, hidden), F32)
    for f in range(fluxes):
        spread = jnp.where(at == f, fmap[f : f + 1, :].astype(F32) * 0.5, spread)
    for r in range(rows):
        share = jnp.zeros((128, 128), F32)
        row = where[1] * rows + r
        for m in range(table.shape[0]):
            local = table[m, where[0], row] - (where[1] - 1) * rows
            share += jnp.where(sublane((128, 128)) // fluxes == local, margin[m, where[0], row], 0.0)
        share = jnp.concatenate([share] * (hidden // 128), axis=1)
        force_ref[r] = (share * spread).astype(BF)
    even = where[1] % 2 == 0
    channels = x_ref.shape[2]
    pick = (lane((rows, 128)) // fluxes == sublane((rows, 128))).astype(BF)
    wet = jnp.where(where[0] == 1, wets[...].astype(F32), 1.0).astype(BF)
    mask = lax.dot_general(wet, pick, (((0,), (0,)), ((), ())), preferred_element_type=F32)
    mask_ref[...] = mask.astype(BF)
    spread = (lane((fluxes, 128)) % fluxes == sublane((fluxes, 128))).astype(BF)
    tiled = lax.dot_general(
        proj[...], spread, (((0,), (0,)), ((), ())), preferred_element_type=F32
    ).astype(BF)
    owner = lane((channels, 128)) // fluxes
    total = None
    for k in range(rows // 2):
        halves = [jnp.where(owner == 2 * k + e, tiled, jnp.zeros_like(tiled)) for e in (0, 1)]
        loads[k].wait()
        if k == 0:
            inner = pltpu.make_async_copy(w_ref.at[where[0]], wv_ref, sems.at[rows // 2 + 5])
            inner.start()
        both = jnp.concatenate([xv_ref[2 * k], xv_ref[2 * k + 1]], axis=1)
        mixed = jnp.concatenate(halves, axis=0)
        fields = jnp.concatenate([dot(both[: lon // 2], mixed), dot(both[lon // 2 :], mixed)], axis=0)
        total = fields if total is None else total + fields
    total = total * mask
    packed = jnp.zeros((group, 128), F32)
    for g in range(GROUPS):
        size = min(group, lon - g * group)
        part = total[g * group : g * group + size]
        if size < group:
            part = jnp.concatenate([part, jnp.zeros((group - size, 128), F32)], axis=0)
        packed += pltpu.roll(part, rows * fluxes * g, 1) if g else part
    packed = packed.astype(BF)
    out_ref[...] = packed
    pair_ref[0:lon, :] = xv_ref[jnp.where(even, rows - 1, 0)]
    pair_ref[lon : lon + group, :] = packed
    chip_ref[...] = xv_ref[jnp.where(even, 0, rows - 1)]
    inner.wait()


def in_hbm(x):
    return pltpu.with_memory_space_constraint(x, pltpu.HBM)


def held():
    return pl.BlockSpec(memory_space=pltpu.VMEM)


def surfaces(where, state, surface_proj, wet_mask, forcing_in, table, weights, inner_weight, group):
    depth, hidden = inner_weight.shape[1:]
    rows, lon, channels = state.shape
    fluxes = surface_proj.shape[2]
    return pl.pallas_call(
        functools.partial(surface_kernel, rows, lon, group, fluxes),
        grid_spec=pltpu.PrefetchScalarGridSpec(
            num_scalar_prefetch=1,
            grid=(1,),
            in_specs=[pl.BlockSpec(memory_space=pltpu.HBM)] * 7,
            out_specs=[held()] * 7,
            scratch_shapes=[
                pltpu.VMEM((fluxes, channels), BF),
                pltpu.VMEM((rows, lon), jnp.int32),
                pltpu.VMEM((fluxes, hidden), BF),
                pltpu.SMEM(table.shape, jnp.int32),
                pltpu.SMEM(table.shape, F32),
                pltpu.SemaphoreType.DMA((rows // 2 + 6,)),
            ],
        ),
        out_shape=[
            pltpu.VMEM((group, 128), BF),
            pltpu.VMEM((rows, lon, channels), BF),
            pltpu.VMEM((lon + group, channels), BF),
            pltpu.VMEM((lon, channels), BF),
            pltpu.VMEM((lon, 128), BF),
            pltpu.VMEM((rows, 128, hidden), BF),
            pltpu.VMEM((depth, hidden), BF),
        ],
        compiler_params=limits(16),
        name="surface_fields",
    )(
        where,
        *[
            in_hbm(x)
            for x in (
                state, jnp.swapaxes(surface_proj, 1, 2), wet_mask, forcing_in, table, weights, inner_weight
            )
        ],
    )


def partial_kernel(pairs, lon, x_ref, w_ref, out_ref, we, wy, wm, tf):
    def tap(a, b):
        return w_ref[(a * 3 + b) * 128 : (a * 3 + b + 1) * 128, :].astype(F32) * 0.5

    for k, (a, b) in enumerate(((0, 0), (0, 2), (1, 1), (2, 1))):
        wy[0, k * 128 : (k + 1) * 128, :] = tap(a, b).astype(BF)
    for k, (a, b) in enumerate(((2, 0), (2, 2), (0, 1), (1, 1))):
        wy[1, k * 128 : (k + 1) * 128, :] = tap(a, b).astype(BF)
    for k, b in enumerate((0, 2)):
        ends = tap(0, b) + tap(2, b)
        wm[0, k * 128 : (k + 1) * 128, :] = (0.5 * (ends + tap(1, b))).astype(BF)
        wm[1, k * 128 : (k + 1) * 128, :] = (0.5 * (ends - tap(1, b))).astype(BF)
    for e, a in enumerate((0, 2)):
        for k, b in enumerate((0, 2, 1)):
            we[e, k * 128 : (k + 1) * 128, :] = tap(a, b).astype(BF)

    for pair in range(pairs):
        slot = pair % tf.shape[0]
        own = [x_ref[2 * pair], x_ref[2 * pair + 1]]
        x1, x2 = own[0].astype(F32), own[1].astype(F32)
        low = x_ref[2 * pair - 1].astype(F32) - x2 if pair else -x2
        high = x_ref[2 * pair + 2].astype(F32) - x1 if pair < pairs - 1 else -x1
        for p, t in enumerate((low, x1 + x2, x2 - x1, high)):
            tf[slot, p, 8 : 8 + lon, :] = t
            tf[slot, p, 7:8, :] = t[lon - 1 : lon]
            tf[slot, p, 8 + lon : 9 + lon, :] = t[0:1]

        def sides(p):
            return [tf[slot, p, 7 : 7 + lon, :].astype(BF), tf[slot, p, 9 : 9 + lon, :].astype(BF)]

        m1 = dot(jnp.concatenate(sides(1), axis=1), wm[0])
        y0 = dot(jnp.concatenate(sides(0) + own, axis=1), wy[0]) + m1
        y1 = dot(jnp.concatenate(sides(3) + own, axis=1), wy[1]) + m1
        m2 = dot(jnp.concatenate(sides(2), axis=1), wm[1])
        out_ref[2 * pair] = (y0 + m2).astype(BF)
        out_ref[2 * pair + 1] = (y1 - m2).astype(BF)


def partials(xv, inner):
    rows, lon, channels = xv.shape
    hidden = inner.shape[1]
    return pl.pallas_call(
        functools.partial(partial_kernel, rows // 2, lon),
        in_specs=[held()] * 2,
        out_specs=[held()] * 2,
        scratch_shapes=[
            pltpu.VMEM((2, 4 * channels, hidden), BF),
            pltpu.VMEM((2, 2 * channels, hidden), BF),
            pltpu.VMEM((1, 4, lon + 16, channels), F32),
        ],
        out_shape=[
            pltpu.VMEM((rows, lon, hidden), BF),
            pltpu.VMEM((2, 3 * channels, hidden), BF),
        ],
        compiler_params=pltpu.CompilerParams(vmem_limit_bytes=26 << 20),
        cost_estimate=pl.CostEstimate(
            flops=rows * lon * 6 * channels * hidden * 2,
            bytes_accessed=rows * lon * (hidden + 2 * channels) * 2,
            transcendentals=0,
        ),
        name="own_rows",
    )(xv, inner)


def finish_kernel(
    rows, lon, group, fluxes, where, x_ref, part_ref, taps_ref, force_ref, mask_ref, pair_ref, chip_ref, near_ref, far_ref,
    o_ref, out_ref, halo, window, done, sems,
):
    even = where[1] % 2 == 0
    center = near_ref[0:group, :].astype(F32)
    other = near_ref[group : 2 * group, :].astype(F32)
    far = far_ref[...].astype(F32)
    packs = [jnp.where(even, far, other), center, jnp.where(even, other, far)]
    for g in range(GROUPS):
        size = min(group, lon - g * group)
        owner = lane((group, 128)) // (rows * fluxes)
        total = jnp.zeros((group, 128), F32)
        for w, pack in enumerate(packs):
            shift = (rows * fluxes * (w - g)) % 128
            moved = pltpu.roll(pack, shift, 1) if shift else pack
            total = jnp.where(owner == w, moved, total)
        window[g * group : g * group + size, :] = total[0:size].astype(BF)
    copies = []
    for r in list(range(1, rows - 1)) + [0, rows - 1]:
        parity = r % 2
        edge = r in (0, rows - 1)
        base = 0 if edge else 256
        if r == 0:
            swap = pair_ref[0:lon, :].astype(F32)
            chip = chip_ref[...].astype(F32)
            for e, v in enumerate((jnp.where(even, chip, swap), jnp.where(even, swap, chip))):
                halo[e, 8 : 8 + lon, :] = v
                halo[e, 7:8, :] = v[lon - 1 : lon]
                halo[e, 8 + lon : 9 + lon, :] = v[0:1]
        if edge:
            lhs = [halo[parity, k : k + lon, :].astype(BF) for k in (7, 9, 8)]
        else:
            lhs = [x_ref[r + 1 if parity else r - 1]]
        total = dot(jnp.concatenate(lhs + [window[...]], axis=1), jnp.concatenate([taps_ref[parity, base:, :], force_ref[r]], axis=0))
        total = (total + part_ref[r].astype(F32)).astype(ACT)
        act = (total + total * jnp.tanh(total)).astype(BF)
        value = x_ref[r].astype(F32) + dot(act, o_ref[0])
        keep = jnp.broadcast_to(mask_ref[:, fluxes * r : fluxes * r + 1], value.shape)
        done[r] = value.astype(BF) * keep
        copy = pltpu.make_async_copy(done.at[r], out_ref.at[r], sems.at[r])
        copy.start()
        copies.append(copy)
    for copy in copies:
        copy.wait()


def finish(where, xv, part, taps, force, mask, received, outer_weight, fluxes):
    rows, lon, channels = xv.shape
    hidden = part.shape[2]
    group = received[3].shape[0]
    return pl.pallas_call(
        functools.partial(finish_kernel, rows, lon, group, fluxes),
        grid_spec=pltpu.PrefetchScalarGridSpec(
            num_scalar_prefetch=1,
            grid=(1,),
            in_specs=[held()] * 9 + [
                pl.BlockSpec((1, hidden, channels), lambda r, s: (s[0], 0, 0)),
            ],
            out_specs=pl.BlockSpec(memory_space=pltpu.HBM),
            scratch_shapes=[
                pltpu.VMEM((2, lon + 16, channels), F32),
                pltpu.VMEM((lon, 128), BF),
                pltpu.VMEM((rows, lon, channels), BF),
                pltpu.SemaphoreType.DMA((rows,)),
            ],
        ),
        out_shape=jax.ShapeDtypeStruct((rows, lon, channels), BF),
        compiler_params=limits(20),
        name="finish_rows",
    )(
        where, xv, part, taps, force, mask, *received, outer_weight
    )


def shards(state, inner_weight, outer_weight, surface_proj, forcing_in, margin_rows, margin_weights, wet_mask):
    count = lax.axis_size("lat")
    half = count // 2
    quarter = half // 2
    lon = state.shape[1]
    group = -(-lon // (GROUPS * 128)) * 128
    moved = (lax.axis_index("lat") + quarter) % count
    where = jnp.where(lax.iota(jnp.int32, 2) == 0, moved // half, moved % half)

    def component(i):
        return ((i + quarter) % count) // half

    def send(block, target):
        return lax.ppermute(block, "lat", [(i, target(i) % count) for i in range(count)])

    pack, xv, pair, chip, mask, force, inner = surfaces(
        where, state, surface_proj, wet_mask, forcing_in, jnp.transpose(margin_rows, (2, 0, 1)),
        jnp.transpose(margin_weights, (2, 0, 1)), inner_weight, group,
    )
    pair = send(pair, lambda i: i + 1 - 2 * (i % 2))
    links = [(i, (i + (1 if i % 2 else -1)) % count) for i in range(count)]
    far = send(pack, lambda i: i + half + (1 if i % 2 else -1))
    near = jnp.concatenate([pack, pair[lon:]], axis=0)
    near, chip = lax.optimization_barrier((near, chip))
    near = send(near, lambda i: i + half)
    chip = lax.ppermute(chip, "lat", [(i, j) for i, j in links if component(i) == component(j)])
    part, taps = partials(xv, inner)
    return finish(where, xv, part, taps, force, mask, (pair, chip, near, far), outer_weight, forcing_in.shape[1])


def solution(mesh):
    placed = (P(("ens", "lat"), None, None), P(), P(), P(), P(), P(), P(), P())
    return jax.shard_map(
        shards, mesh=mesh, in_specs=placed, out_specs=P(("ens", "lat"), None, None), check_vma=False
    )
```

```python
import functools

import jax
import jax.numpy as jnp
from jax import lax
from jax.experimental import pallas as pl
from jax.experimental.pallas import tpu as pltpu
from jax.sharding import PartitionSpec as P

BF = jnp.bfloat16
F32 = jnp.float32
ACT = BF
GROUPS = 4


def dot(a, b):
    return jnp.dot(a, b, preferred_element_type=F32)


def lane(shape):
    return lax.broadcasted_iota(jnp.int32, shape, len(shape) - 1)


def sublane(shape):
    return lax.broadcasted_iota(jnp.int32, shape, len(shape) - 2)


def limits(mib):
    return pltpu.CompilerParams(
        dimension_semantics=("arbitrary",), vmem_limit_bytes=mib << 20
    )


def surface_kernel(
    rows, lon, group, fluxes, where, x_ref, proj_ref, wet_ref, f_ref, table_ref, margin_ref, w_ref, out_ref,
    xv_ref, pair_ref, chip_ref, mask_ref, force_ref, wv_ref, proj, wets, fmap, table, margin, sems,
):
    def load(k):
        both = pl.ds(2 * k, 2)
        copy = pltpu.make_async_copy(x_ref.at[both], xv_ref.at[both], sems.at[k])
        copy.start()
        return copy

    loads = [load(0)]
    small = [
        pltpu.make_async_copy(proj_ref.at[where[0]], proj, sems.at[rows // 2]),
        pltpu.make_async_copy(
            wet_ref.at[pl.ds(pl.multiple_of(where[1] * rows, rows), rows)], wets, sems.at[rows // 2 + 1]
        ),
        pltpu.make_async_copy(f_ref.at[where[0]], fmap, sems.at[rows // 2 + 2]),
        pltpu.make_async_copy(table_ref, table, sems.at[rows // 2 + 3]),
        pltpu.make_async_copy(margin_ref, margin, sems.at[rows // 2 + 4]),
    ]
    for copy in small:
        copy.start()
    loads += [load(k) for k in range(1, rows // 2)]
    for copy in small:
        copy.wait()
    hidden = fmap.shape[1]
    at = sublane((128, hidden)) % fluxes
    spread = jnp.zeros((128, hidden), F32)
    for f in range(fluxes):
        spread = jnp.where(at == f, fmap[f : f + 1, :].astype(F32) * 0.5, spread)
    for r in range(rows):
        share = jnp.zeros((128, 128), F32)
        row = where[1] * rows + r
        for m in range(table.shape[0]):
            local = table[m, where[0], row] - (where[1] - 1) * rows
            share += jnp.where(sublane((128, 128)) // fluxes == local, margin[m, where[0], row], 0.0)
        share = jnp.concatenate([share] * (hidden // 128), axis=1)
        force_ref[r] = (share * spread).astype(BF)
    even = where[1] % 2 == 0
    channels = x_ref.shape[2]
    pick = (lane((rows, 128)) // fluxes == sublane((rows, 128))).astype(BF)
    wet = jnp.where(where[0] == 1, wets[...].astype(F32), 1.0).astype(BF)
    mask = lax.dot_general(wet, pick, (((0,), (0,)), ((), ())), preferred_element_type=F32)
    mask_ref[...] = mask.astype(BF)
    spread = (lane((fluxes, 128)) % fluxes == sublane((fluxes, 128))).astype(BF)
    tiled = lax.dot_general(
        proj[...], spread, (((0,), (0,)), ((), ())), preferred_element_type=F32
    ).astype(BF)
    owner = lane((channels, 128)) // fluxes
    total = None
    for k in range(rows // 2):
        halves = [jnp.where(owner == 2 * k + e, tiled, jnp.zeros_like(tiled)) for e in (0, 1)]
        loads[k].wait()
        if k == 0:
            inner = pltpu.make_async_copy(w_ref.at[where[0]], wv_ref, sems.at[rows // 2 + 5])
            inner.start()
        both = jnp.concatenate([xv_ref[2 * k], xv_ref[2 * k + 1]], axis=1)
        mixed = jnp.concatenate(halves, axis=0)
        fields = jnp.concatenate([dot(both[: lon // 2], mixed), dot(both[lon // 2 :], mixed)], axis=0)
        total = fields if total is None else total + fields
    total = total * mask
    packed = jnp.zeros((group, 128), F32)
    for g in range(GROUPS):
        size = min(group, lon - g * group)
        part = total[g * group : g * group + size]
        if size < group:
            part = jnp.concatenate([part, jnp.zeros((group - size, 128), F32)], axis=0)
        packed += pltpu.roll(part, rows * fluxes * g, 1) if g else part
    packed = packed.astype(BF)
    out_ref[...] = packed
    pair_ref[...] = xv_ref[jnp.where(even, rows - 1, 0)]
    chip_ref[...] = xv_ref[jnp.where(even, 0, rows - 1)]
    inner.wait()


def in_hbm(x):
    return pltpu.with_memory_space_constraint(x, pltpu.HBM)


def held():
    return pl.BlockSpec(memory_space=pltpu.VMEM)


def surfaces(where, state, surface_proj, wet_mask, forcing_in, table, weights, inner_weight, group):
    depth, hidden = inner_weight.shape[1:]
    rows, lon, channels = state.shape
    fluxes = surface_proj.shape[2]
    return pl.pallas_call(
        functools.partial(surface_kernel, rows, lon, group, fluxes),
        grid_spec=pltpu.PrefetchScalarGridSpec(
            num_scalar_prefetch=1,
            grid=(1,),
            in_specs=[pl.BlockSpec(memory_space=pltpu.HBM)] * 7,
            out_specs=[held()] * 7,
            scratch_shapes=[
                pltpu.VMEM((fluxes, channels), BF),
                pltpu.VMEM((rows, lon), jnp.int32),
                pltpu.VMEM((fluxes, hidden), BF),
                pltpu.SMEM(table.shape, jnp.int32),
                pltpu.SMEM(table.shape, F32),
                pltpu.SemaphoreType.DMA((rows // 2 + 6,)),
            ],
        ),
        out_shape=[
            pltpu.VMEM((group, 128), BF),
            pltpu.VMEM((rows, lon, channels), BF),
            pltpu.VMEM((lon, channels), BF),
            pltpu.VMEM((lon, channels), BF),
            pltpu.VMEM((lon, 128), BF),
            pltpu.VMEM((rows, 128, hidden), BF),
            pltpu.VMEM((depth, hidden), BF),
        ],
        compiler_params=limits(16),
        name="surface_fields",
    )(
        where,
        *[
            in_hbm(x)
            for x in (
                state, jnp.swapaxes(surface_proj, 1, 2), wet_mask, forcing_in, table, weights, inner_weight
            )
        ],
    )


def partial_kernel(pairs, lon, x_ref, w_ref, out_ref, we, wy, wm, tf):
    def tap(a, b):
        return w_ref[(a * 3 + b) * 128 : (a * 3 + b + 1) * 128, :].astype(F32) * 0.5

    for k, (a, b) in enumerate(((0, 0), (0, 2), (1, 1), (2, 1))):
        wy[0, k * 128 : (k + 1) * 128, :] = tap(a, b).astype(BF)
    for k, (a, b) in enumerate(((2, 0), (2, 2), (0, 1), (1, 1))):
        wy[1, k * 128 : (k + 1) * 128, :] = tap(a, b).astype(BF)
    for k, b in enumerate((0, 2)):
        ends = tap(0, b) + tap(2, b)
        wm[0, k * 128 : (k + 1) * 128, :] = (0.5 * (ends + tap(1, b))).astype(BF)
        wm[1, k * 128 : (k + 1) * 128, :] = (0.5 * (ends - tap(1, b))).astype(BF)
    for e, a in enumerate((0, 2)):
        for k, b in enumerate((0, 2, 1)):
            we[e, k * 128 : (k + 1) * 128, :] = tap(a, b).astype(BF)

    for pair in range(pairs):
        slot = pair % tf.shape[0]
        own = [x_ref[2 * pair], x_ref[2 * pair + 1]]
        x1, x2 = own[0].astype(F32), own[1].astype(F32)
        low = x_ref[2 * pair - 1].astype(F32) - x2 if pair else -x2
        high = x_ref[2 * pair + 2].astype(F32) - x1 if pair < pairs - 1 else -x1
        for p, t in enumerate((low, x1 + x2, x2 - x1, high)):
            tf[slot, p, 8 : 8 + lon, :] = t
            tf[slot, p, 7:8, :] = t[lon - 1 : lon]
            tf[slot, p, 8 + lon : 9 + lon, :] = t[0:1]

        def sides(p):
            return [tf[slot, p, 7 : 7 + lon, :].astype(BF), tf[slot, p, 9 : 9 + lon, :].astype(BF)]

        m1 = dot(jnp.concatenate(sides(1), axis=1), wm[0])
        m2 = dot(jnp.concatenate(sides(2), axis=1), wm[1])
        out_ref[2 * pair] = (dot(jnp.concatenate(sides(0) + own, axis=1), wy[0]) + (m1 + m2)).astype(BF)
        out_ref[2 * pair + 1] = (dot(jnp.concatenate(sides(3) + own, axis=1), wy[1]) + (m1 - m2)).astype(BF)


def partials(xv, inner):
    rows, lon, channels = xv.shape
    hidden = inner.shape[1]
    return pl.pallas_call(
        functools.partial(partial_kernel, rows // 2, lon),
        in_specs=[held()] * 2,
        out_specs=[held()] * 2,
        scratch_shapes=[
            pltpu.VMEM((2, 4 * channels, hidden), BF),
            pltpu.VMEM((2, 2 * channels, hidden), BF),
            pltpu.VMEM((1, 4, lon + 16, channels), F32),
        ],
        out_shape=[
            pltpu.VMEM((rows, lon, hidden), BF),
            pltpu.VMEM((2, 3 * channels, hidden), BF),
        ],
        compiler_params=pltpu.CompilerParams(vmem_limit_bytes=26 << 20),
        cost_estimate=pl.CostEstimate(
            flops=rows * lon * 6 * channels * hidden * 2,
            bytes_accessed=rows * lon * (hidden + 2 * channels) * 2,
            transcendentals=0,
        ),
        name="own_rows",
    )(xv, inner)


def finish_kernel(
    rows, lon, group, fluxes, where, x_ref, part_ref, taps_ref, force_ref, mask_ref, pair_ref, chip_ref, near_ref, far_ref,
    o_ref, out_ref, halo, window, done, sems,
):
    even = where[1] % 2 == 0
    center = near_ref[0:group, :].astype(F32)
    other = near_ref[group : 2 * group, :].astype(F32)
    far = far_ref[...].astype(F32)
    packs = [jnp.where(even, far, other), center, jnp.where(even, other, far)]
    for g in range(GROUPS):
        size = min(group, lon - g * group)
        owner = lane((group, 128)) // (rows * fluxes)
        total = jnp.zeros((group, 128), F32)
        for w, pack in enumerate(packs):
            shift = (rows * fluxes * (w - g)) % 128
            moved = pltpu.roll(pack, shift, 1) if shift else pack
            total = jnp.where(owner == w, moved, total)
        window[g * group : g * group + size, :] = total[0:size].astype(BF)
    copies = []
    for r in list(range(1, rows - 1)) + [0, rows - 1]:
        parity = r % 2
        edge = r in (0, rows - 1)
        base = 0 if edge else 256
        if r == 0:
            swap = pair_ref[...].astype(F32)
            chip = chip_ref[...].astype(F32)
            for e, v in enumerate((jnp.where(even, chip, swap), jnp.where(even, swap, chip))):
                halo[e, 8 : 8 + lon, :] = v
                halo[e, 7:8, :] = v[lon - 1 : lon]
                halo[e, 8 + lon : 9 + lon, :] = v[0:1]
        if edge:
            lhs = [halo[parity, k : k + lon, :].astype(BF) for k in (7, 9, 8)]
        else:
            lhs = [x_ref[r + 1 if parity else r - 1]]
        total = dot(jnp.concatenate(lhs + [window[...]], axis=1), jnp.concatenate([taps_ref[parity, base:, :], force_ref[r]], axis=0))
        total = (total + part_ref[r].astype(F32)).astype(ACT)
        act = (total + total * jnp.tanh(total)).astype(BF)
        value = x_ref[r].astype(F32) + dot(act, o_ref[0])
        keep = jnp.broadcast_to(mask_ref[:, fluxes * r : fluxes * r + 1], value.shape)
        done[r] = value.astype(BF) * keep
        copy = pltpu.make_async_copy(done.at[r], out_ref.at[r], sems.at[r])
        copy.start()
        copies.append(copy)
    for copy in copies:
        copy.wait()


def finish(where, xv, part, taps, force, mask, received, outer_weight, fluxes):
    rows, lon, channels = xv.shape
    hidden = part.shape[2]
    group = received[3].shape[0]
    return pl.pallas_call(
        functools.partial(finish_kernel, rows, lon, group, fluxes),
        grid_spec=pltpu.PrefetchScalarGridSpec(
            num_scalar_prefetch=1,
            grid=(1,),
            in_specs=[held()] * 9 + [
                pl.BlockSpec((1, hidden, channels), lambda r, s: (s[0], 0, 0)),
            ],
            out_specs=pl.BlockSpec(memory_space=pltpu.HBM),
            scratch_shapes=[
                pltpu.VMEM((2, lon + 16, channels), F32),
                pltpu.VMEM((lon, 128), BF),
                pltpu.VMEM((rows, lon, channels), BF),
                pltpu.SemaphoreType.DMA((rows,)),
            ],
        ),
        out_shape=jax.ShapeDtypeStruct((rows, lon, channels), BF),
        compiler_params=limits(20),
        name="finish_rows",
    )(
        where, xv, part, taps, force, mask, *received, outer_weight
    )


def shards(state, inner_weight, outer_weight, surface_proj, forcing_in, margin_rows, margin_weights, wet_mask):
    count = lax.axis_size("lat")
    half = count // 2
    quarter = half // 2
    lon = state.shape[1]
    group = -(-lon // (GROUPS * 128)) * 128
    moved = (lax.axis_index("lat") + quarter) % count
    where = jnp.where(lax.iota(jnp.int32, 2) == 0, moved // half, moved % half)

    def component(i):
        return ((i + quarter) % count) // half

    def send(block, target):
        return lax.ppermute(block, "lat", [(i, target(i) % count) for i in range(count)])

    pack, xv, pair, chip, mask, force, inner = surfaces(
        where, state, surface_proj, wet_mask, forcing_in, jnp.transpose(margin_rows, (2, 0, 1)),
        jnp.transpose(margin_weights, (2, 0, 1)), inner_weight, group,
    )
    partner = send(pack, lambda i: i + 1 - 2 * (i % 2))
    links = [(i, (i + (1 if i % 2 else -1)) % count) for i in range(count)]
    far = send(pack, lambda i: i + half + (1 if i % 2 else -1))
    near = jnp.concatenate([pack, partner], axis=0)
    near, chip, pair = lax.optimization_barrier((near, chip, pair))
    near = send(near, lambda i: i + half)
    chip = lax.ppermute(chip, "lat", [(i, j) for i, j in links if component(i) == component(j)])
    pair = send(pair, lambda i: i + 1 - 2 * (i % 2))
    part, taps = partials(xv, inner)
    return finish(where, xv, part, taps, force, mask, (pair, chip, near, far), outer_weight, forcing_in.shape[1])


def solution(mesh):
    placed = (P(("ens", "lat"), None, None), P(), P(), P(), P(), P(), P(), P())
    return jax.shard_map(
        shards, mesh=mesh, in_specs=placed, out_specs=P(("ens", "lat"), None, None), check_vma=False
    )
```
